512 devices in a mesh: band: 64 (over z, x, core), mem: 8 (over y).
Axes of the slice: x: 4, y: 8, z: 8, core: 2. Of those that a mesh axis runs over, the one named last changes fastest.
Arguments:
- spectra: bfloat16 [16, 4, 2, 2, 901120], P('mem', None, None, None, 'band'), may hold values from -6 to 6
- legendre: bfloat16 [40, 901120], P(None, 'band'), may hold values from -0.0034179688 to 0.0034179688
- pair_waves: int32 [640], P('band'), may hold values from 0 to 639, each once
- band_lengths: int32 [64], replicated, may hold values from 1 to 2, 80 in all
- eof_basis: bfloat16 [128, 2560, 256], P('band'), may hold values from -0.0390625 to 0.0390625
Outputs:
- grid_fields: bfloat16 [16, 4, 2, 128, 2560], P('mem', None, None, 'band')
- eof_coeffs: float32 [16, 4, 2, 256], P('mem', None, None, 'band')
The draws below stay inside these ranges and needn't reach their ends.
Inputs may be any that keep to these rules, and one draw needn't show every extreme that they name: `pair_waves`: every lower wavenumber 0 .. 639 stands in exactly one pair slot. `band_lengths`: the lengths sum to 80; some band has exactly 2 rows.
All inputs are finite; a program needn't handle non-finite values.
Results may differ from the reference program's by a relative error of at most 0.0055.
Values may be sent and summed in bfloat16 or wider, within the bound.
No kernel may reach another device: no remote copies, remote signals or barrier semaphores. Data moves between devices by JAX's collectives and lax.ppermute only.
A program may use at most 192 MiB of HBM per device.

```python
import math
from functools import partial
import jax
import jax.numpy as jnp
import numpy as np
from jax import lax

WAVE_COUNT = 1280
LON = 2560
NEOF = 256
FIELD_COUNT = 4
LEVEL_COUNT = 2
LMAX = 2
BLK = 128
MEMBER_COUNT = 16
BANDS = 64
LAT = 80
HALF_LATITUDES = 40
PAIR_LEN = 1408
SLOT_TOTAL = 901120
LSLOTS = 128


def raised(entries, own_key, source, target, parts, factor):
    def block_of(axis_at):
        return (jnp.arange(entries.shape[axis_at]) // (entries.shape[axis_at] // parts)).reshape((-1,) + (1,) * (entries.ndim - 1 - axis_at))

    one_side = jax.random.permutation(own_key, parts)[block_of(target)]
    far = (block_of(target) + parts // 2) % parts
    return jnp.where((block_of(source) == one_side) | (block_of(source) == far), factor * entries, entries)


def level_of(rng, shape, shards, least, largest):
    factor_of, own = 1.0, jax.random.fold_in(rng, 6)
    for axis_at, parts in shards:
        heights = jnp.exp(jax.random.uniform(jax.random.fold_in(own, axis_at), (parts,), jnp.float32, least / len(shards), largest / len(shards)))
        factor_of = factor_of * jnp.repeat(heights, shape[axis_at] // parts).reshape([-1 if axis == axis_at else 1 for axis in range(len(shape))])
    return factor_of


def split_up(amount, total, bound, slope):
    weights = [(1 << 20) // math.isqrt(grade ** slope) + 1 for grade in range(2, amount + 1)]
    surplus, holding = total - bound - (amount - 1), [1] * (amount - 1)
    while surplus > 0:
        free = [i for i in range(amount - 1) if holding[i] < bound]
        whole, remaining = sum([weights[i] for i in free]), surplus
        for i in free:
            extra = min(bound - holding[i], max(1, remaining * weights[i] // whole), surplus)
            holding[i] = holding[i] + extra
            surplus = surplus - extra
    return np.array([bound] + holding)


def ragged(rng, amount, total, most, lean):
    if amount == 2:
        one = jax.random.randint(rng, (), max(1, total - most), min(most, total - 1) + 1)
        return jnp.stack([one, total - one])
    tallies = jnp.asarray(split_up(amount, total, most, lean), jnp.int32)
    twos = (amount - 1) // 2
    donor, sink = tallies[1:1 + 2 * twos:2], tallies[2:2 + 2 * twos:2]
    room = jnp.minimum(donor - 1, most - sink)
    passed = jax.random.randint(jax.random.fold_in(rng, 1), (twos,), 0, 1 << 20) % (room + 1)
    tallies = tallies.at[1:1 + 2 * twos:2].set(donor - passed).at[2:2 + 2 * twos:2].set(sink + passed)
    return tallies[jax.random.permutation(jax.random.fold_in(rng, 2), amount)]


def scatter_about(stream_key, dims, width, bound, split=(), held_as=jnp.bfloat16):
    values = width * jax.random.normal(stream_key, dims, jnp.float32)
    if split:
        values = values * level_of(stream_key, dims, split, -0.22, 0.18)
    return jnp.clip(values, -bound, bound).astype(held_as)


def heavy_noise(key, shape, width, bound, split, heavy, kind=jnp.bfloat16):
    entries = width * jax.random.normal(key, shape, jnp.float32)
    if split:
        entries = entries * level_of(key, shape, split, -0.22, 0.18)
    return jnp.clip(raised(entries, jax.random.fold_in(key, 3), *heavy), -bound, bound).astype(kind)


def setup_inputs(seed: int = 0) -> dict:
    seeds = jax.random.split(jax.random.key(seed), 6)
    spectra = scatter_about(seeds[0], (MEMBER_COUNT, FIELD_COUNT, LEVEL_COUNT, 2, SLOT_TOTAL), 1.0, 6.0, ((0, 8), (4, 64)))
    legendre = scatter_about(seeds[1], (HALF_LATITUDES, SLOT_TOTAL), (2 * WAVE_COUNT * WAVE_COUNT) ** -0.5, 0.0034179688, ((1, 64),))
    pair_waves = jax.random.permutation(seeds[2], WAVE_COUNT // 2).astype(jnp.int32)
    band_lengths = ragged(seeds[3], BANDS, LAT, LMAX, 2).astype(jnp.int32)
    eof_basis = heavy_noise(seeds[4], (LSLOTS, LON, NEOF), (LAT * LON) ** -0.5, 0.0390625, ((0, 64),), (0, 2, 64, 4.0))
    return dict(spectra=spectra, legendre=legendre, pair_waves=pair_waves, band_lengths=band_lengths, eof_basis=eof_basis)


def wave_table(orders, length):
    lon_index = jnp.arange(length, dtype=jnp.int32)
    phase_idx = (orders[..., None] * lon_index) % length
    angle_rad = phase_idx.astype(jnp.float32) * (2.0 * math.pi / length)
    weight = jnp.where(orders == 0, 1.0, 2.0).astype(jnp.float32)[..., None]
    return jnp.stack([weight * jnp.cos(angle_rad), -weight * jnp.sin(angle_rad)]).astype(jnp.bfloat16)


def pair_fourier(flat_spectral_coeffs, legendre, pair_waves, pair_slot):
    slot_start = (pair_slot * PAIR_LEN).astype(jnp.int32)
    coeffs = lax.dynamic_slice_in_dim(flat_spectral_coeffs, slot_start, PAIR_LEN, 1).astype(jnp.float32)
    rows_tab = lax.dynamic_slice_in_dim(legendre, slot_start, PAIR_LEN, 1).astype(jnp.float32)
    lower_wave = pair_waves[pair_slot]
    position = jnp.arange(PAIR_LEN, dtype=jnp.int32)
    low_blocks = WAVE_COUNT // BLK - lower_wave // BLK
    upper_pos = position - low_blocks * BLK
    low_mask = (position < WAVE_COUNT - lower_wave).astype(jnp.float32)
    high_mask = ((upper_pos >= 0) & (upper_pos < lower_wave + 1)).astype(jnp.float32)
    alternate = jnp.where(position % 2 == 0, 1.0, -1.0).astype(jnp.float32)
    south_tab = rows_tab * alternate
    outputs = []
    for mask_row in (low_mask, high_mask):
        masked = coeffs * mask_row
        north_part = jnp.dot(masked, rows_tab.T, precision=lax.Precision.HIGHEST)
        south_part = jnp.dot(masked, south_tab.T, precision=lax.Precision.HIGHEST)
        outputs.append(jnp.concatenate([north_part, south_part[:, ::-1]], axis=1))
    return jnp.stack(outputs)


def reference(spectra, legendre, pair_waves, band_lengths, eof_basis):
    flat_spectral_coeffs = spectra.reshape(MEMBER_COUNT * FIELD_COUNT * LEVEL_COUNT * 2, SLOT_TOTAL)
    fourier = lax.map(partial(pair_fourier, flat_spectral_coeffs, legendre, pair_waves), jnp.arange(WAVE_COUNT // 2, dtype=jnp.int32))
    fourier = lax.optimization_barrier(fourier.astype(jnp.bfloat16)).astype(jnp.float32)
    fourier = fourier.reshape(WAVE_COUNT // 2, 2, MEMBER_COUNT, FIELD_COUNT, LEVEL_COUNT, 2, LAT)
    orders = jnp.stack([pair_waves, WAVE_COUNT - 1 - pair_waves], axis=1)
    wave_cos = wave_table(orders, LON).astype(jnp.float32)
    grid_sum = jnp.einsum("phabdcj,cphk->abdjk", fourier, wave_cos, precision=lax.Precision.HIGHEST)
    grid_lat = grid_sum.astype(jnp.bfloat16)
    starts = (jnp.cumsum(band_lengths) - band_lengths).astype(jnp.int32)
    offsets = jnp.arange(LMAX, dtype=jnp.int32)
    row_index = jnp.minimum(starts[:, None] + offsets[None, :], LAT - 1).reshape(-1).astype(jnp.int32)
    row_keep = (offsets[None, :] < band_lengths[:, None]).reshape(-1)
    picked = jnp.take(grid_lat, row_index, axis=3)
    grid_fields = jnp.where(row_keep[:, None], picked, jnp.zeros((), picked.dtype)).astype(jnp.bfloat16)
    flat_grid = grid_fields.reshape(MEMBER_COUNT * FIELD_COUNT * LEVEL_COUNT, LSLOTS * LON)
    projection = jnp.dot(flat_grid, eof_basis.reshape(LSLOTS * LON, NEOF), preferred_element_type=jnp.float32)
    projection = projection.reshape(MEMBER_COUNT, FIELD_COUNT * LEVEL_COUNT, NEOF)
    anomaly = projection - jnp.mean(projection, axis=0, keepdims=True)
    return grid_fields, anomaly.reshape(MEMBER_COUNT, FIELD_COUNT, LEVEL_COUNT, NEOF)
```

```python
import math

import jax
import jax.numpy as jnp
from jax import lax
from jax.sharding import PartitionSpec as P

WAVE_COUNT = 1280
BLK = 128


def wave_block(orders, start, width, length):
    lon_index = start + jnp.arange(width, dtype=jnp.int32)
    phase_idx = orders[..., None] * lon_index % length
    angle_rad = phase_idx.astype(jnp.float32) * (2.0 * math.pi / length)
    weight = jnp.where(orders == 0, 1.0, 2.0).astype(jnp.float32)[..., None]
    return jnp.stack([weight * jnp.cos(angle_rad), -weight * jnp.sin(angle_rad)]).astype(
        jnp.bfloat16
    )


def shards(spectra, legendre, pair_waves, band_lengths, eof_basis):
    ens_dev, fields, level_stack, re_im, slot_count = spectra.shape
    lat_half = legendre.shape[0]
    pairs_dev = pair_waves.shape[0]
    blocks = slot_count // (pairs_dev * BLK)
    columns = ens_dev * fields * level_stack * re_im
    band_count = lax.axis_size("band")
    most_rows, longitudes, eof_modes = eof_basis.shape
    spectral_data = spectra.reshape(columns, pairs_dev, blocks, BLK)
    legendre_rows = legendre.reshape(lat_half, pairs_dev, blocks, BLK)
    position = jnp.arange(blocks * BLK, dtype=jnp.int32).reshape(1, blocks, BLK)
    lower_wave = pair_waves.reshape(pairs_dev, 1, 1)
    low_blocks = WAVE_COUNT // BLK - lower_wave // BLK
    upper_pos = position - low_blocks * BLK
    in_range = (position < WAVE_COUNT - lower_wave) | (upper_pos >= 0) & (
        upper_pos < lower_wave + 1
    )
    spectral_data = spectral_data * in_range.astype(jnp.bfloat16)[None]
    block_index = jnp.arange(blocks, dtype=jnp.int32)[None, :]
    low_owner = (block_index < low_blocks[:, :, 0]).astype(jnp.float32)
    owners = jnp.stack([low_owner, 1.0 - low_owner], axis=1)
    alternate = jnp.where(jnp.arange(BLK) % 2 == 0, 1.0, -1.0).astype(jnp.bfloat16)
    north_part = jnp.einsum(
        "cptk,jptk->ptcj", spectral_data, legendre_rows, preferred_element_type=jnp.float32
    )
    south_part = jnp.einsum(
        "cptk,jptk->ptcj",
        spectral_data,
        legendre_rows * alternate,
        preferred_element_type=jnp.float32,
    )
    rows_all = jnp.concatenate([north_part, south_part[..., ::-1]], axis=-1)
    fourier = jnp.einsum(
        "pht,ptcj->jphc", owners, rows_all, precision=lax.Precision.HIGHEST
    ).astype(jnp.bfloat16)
    starts = jnp.cumsum(band_lengths) - band_lengths
    offsets = jnp.arange(most_rows, dtype=jnp.int32)
    row_index = jnp.minimum(starts[:, None] + offsets[None, :], 2 * lat_half - 1).reshape(-1)
    packed = jnp.take(fourier, row_index, axis=0).reshape(
        band_count, most_rows, pairs_dev * 2 * columns
    )
    arrived = lax.all_to_all(packed, "band", split_axis=0, concat_axis=0, tiled=True)
    all_waves = lax.all_gather(pair_waves, "band", axis=0, tiled=True).reshape(
        band_count, pairs_dev
    )
    lower_all = all_waves.T
    orders = jnp.stack([lower_all, WAVE_COUNT - 1 - lower_all], axis=1)
    arrived = arrived.reshape(
        band_count, most_rows, pairs_dev, 2, ens_dev, fields, level_stack, re_im
    )
    lon_width = math.gcd(longitudes, 512)
    lon_blocks = longitudes // lon_width

    def synth_block(block_number):
        table_part = wave_block(orders, block_number * lon_width, lon_width, longitudes)
        return jnp.einsum(
            "srphabdc,cphsk->abdrk", arrived, table_part, preferred_element_type=jnp.float32
        )

    grid_parts = lax.map(synth_block, jnp.arange(lon_blocks, dtype=jnp.int32))
    grid_sum = jnp.moveaxis(grid_parts, 0, 4).reshape(
        ens_dev, fields, level_stack, most_rows, longitudes
    )
    own_rows = band_lengths[lax.axis_index("band")]
    row_keep = (offsets < own_rows).astype(jnp.float32)
    grid_fields = (grid_sum * row_keep[:, None]).astype(jnp.bfloat16)
    flat_grid = grid_fields.reshape(ens_dev * fields * level_stack, most_rows * longitudes)
    partial_value = jnp.dot(
        flat_grid,
        eof_basis.reshape(most_rows * longitudes, eof_modes),
        preferred_element_type=jnp.float32,
    )
    share_width = eof_modes // band_count
    shares = partial_value.reshape(-1, band_count, share_width).transpose(1, 2, 0)
    shares = lax.all_to_all(shares, "band", split_axis=0, concat_axis=0, tiled=True)
    own_share = jnp.sum(shares, axis=0).T
    local_share = own_share.reshape(ens_dev, fields * level_stack, share_width)
    local_sum = jnp.sum(local_share, axis=0)
    member_groups = lax.axis_size("mem")
    copies = jnp.broadcast_to(local_sum[None], (member_groups, *local_sum.shape))
    summed = jnp.sum(lax.all_to_all(copies, "mem", 0, 0, tiled=True), axis=0)
    anomaly = local_share - summed / (ens_dev * lax.axis_size("mem"))
    return (grid_fields, anomaly.reshape(ens_dev, fields, level_stack, share_width))


def solution(mesh):
    return jax.shard_map(
        shards,
        mesh=mesh,
        in_specs=(
            P("mem", None, None, None, "band"),
            P(None, "band"),
            P("band"),
            P(),
            P("band", None, None),
        ),
        out_specs=(P("mem", None, None, "band", None), P("mem", None, None, "band")),
        check_vma=False,
    )
```

```python
import math

import jax
import jax.numpy as jnp
import numpy as np
from jax import lax
from jax.experimental import pallas as pl
from jax.experimental.pallas import tpu as pltpu
from jax.sharding import PartitionSpec as P

WAVE_COUNT = 1280
LON = 2560
BLK = 128
HALF = 40
BANDS = 64
PAIRS = 10
PAIR_LEN = 1408
FIELDS = 16
RADIX = 10
STEP = LON // RADIX
MODES = 256
SHARE = MODES // BANDS
SLOT_ROWS = 16
LOWS = WAVE_COUNT // 2
PER_CLASS = LOWS // RADIX
DIGIT = 16
KEEP_LANE = 2 * PAIRS
F32 = jnp.float32
BF16 = jnp.bfloat16


def wave_table():
    ladder = RADIX * np.arange(PER_CLASS)
    parts = []
    for c in range(RADIX):
        low = ladder + c
        high = WAVE_COUNT - RADIX - ladder + c
        orders = np.concatenate([low, high] if c % 2 == 0 else [high, low])
        phase = orders[:, None] * np.arange(STEP)[None, :] % LON
        angle = phase.astype(np.float32) * np.float32(2.0 * math.pi / LON)
        weight = np.where(orders == 0, 1.0, 2.0).astype(np.float32)[:, None]
        parts.append(np.concatenate([weight * np.cos(angle), -weight * np.sin(angle)]))
    return np.stack(parts).astype(jnp.bfloat16)


def legendre_kernel(
    waves, lengths, spectra_hbm, legendre_hbm, out, spectra_buf, legendre_buf, flat, sems
):
    def fetch(p):
        window = pl.ds(p * PAIR_LEN, PAIR_LEN)
        return (
            pltpu.make_async_copy(
                spectra_hbm.at[:, :, window], spectra_buf.at[p], sems.at[0, p]
            ),
            pltpu.make_async_copy(
                legendre_hbm.at[:, window], legendre_buf.at[p], sems.at[1, p]
            ),
        )

    for p in range(PAIRS):
        for copy in fetch(p):
            copy.start()
    counts = lengths[...].astype(F32)
    dest = lax.broadcasted_iota(jnp.int32, (BANDS, BANDS), 0)
    other = lax.broadcasted_iota(jnp.int32, (BANDS, BANDS), 1)
    starts = jnp.sum(jnp.where(other < dest, counts, 0.0), axis=1, keepdims=True)
    own = jnp.sum(jnp.where(other == dest, counts, 0.0), axis=1, keepdims=True)
    column = lax.broadcasted_iota(jnp.int32, (BANDS, 2 * HALF), 1).astype(F32)
    picks = []
    for r in range(2):
        row = jnp.minimum(starts + r, 2 * HALF - 1.0)
        source = jnp.where(row < HALF, row, 3 * HALF - 1.0 - row)
        picks.append((column == source).astype(BF16))
    pick = jnp.concatenate(picks, axis=0)
    lane = lax.broadcasted_iota(jnp.int32, (BANDS, BLK), 1)
    notes = jnp.where(lane == KEEP_LANE, jnp.where(own > 1.0, 1.0, 0.0), 0.0)
    position = lax.broadcasted_iota(jnp.int32, (FIELDS, PAIR_LEN), 1)
    parity = lax.broadcasted_iota(jnp.int32, (HALF, PAIR_LEN), 1) % 2
    alternate = jnp.where(parity == 0, 1.0, -1.0).astype(BF16)
    flat[...] = jnp.zeros(flat.shape, F32)
    for p in range(PAIRS):
        wave = waves[p]
        place = (wave % RADIX) * PER_CLASS + wave // RADIX
        notes = jnp.where(lane == p, (place // DIGIT).astype(F32), notes)
        notes = jnp.where(lane == PAIRS + p, (place % DIGIT).astype(F32), notes)
        upper = position - (WAVE_COUNT // BLK - wave // BLK) * BLK
        low = (position < WAVE_COUNT - wave).astype(F32).astype(BF16)
        high = ((upper >= 0) & (upper < wave + 1)).astype(F32).astype(BF16)
        for copy in fetch(p):
            copy.wait()
        coeffs = spectra_buf[p].reshape(2 * FIELDS, PAIR_LEN)
        halves = [jnp.concatenate([mask, mask], axis=0) * coeffs for mask in (low, high)]
        masked = jnp.concatenate(halves, axis=0)
        north = legendre_buf[p]
        rows = jnp.concatenate([north, north * alternate], axis=0)
        fourier = lax.dot_general(
            rows, masked, (((1,), (1,)), ((), ())), preferred_element_type=F32
        ).astype(BF16)
        picked = jnp.dot(pick, fourier, preferred_element_type=F32)
        flat[pl.ds(p, BANDS, stride=SLOT_ROWS), :] = jnp.concatenate(
            [picked[:BANDS], picked[BANDS:]], axis=1
        )
    flat[pl.ds(PAIRS, BANDS, stride=SLOT_ROWS), :] = notes
    out[...] = flat[...].astype(BF16).reshape(BANDS, SLOT_ROWS, BLK)


def synthesis_kernel(
    arrived, table_hbm, basis_hbm, grid_out, share_out,
    flat, sorted_buf, series, partial_buf, turned, table, basis, sems,
):
    table_copy = pltpu.make_async_copy(table_hbm, table, sems.at[0])
    basis_copy = pltpu.make_async_copy(basis_hbm, basis, sems.at[1])
    table_copy.start()
    basis_copy.start()
    flat[...] = arrived[...].reshape(BANDS * SLOT_ROWS, BLK).astype(F32)
    notes = flat[pl.ds(PAIRS, BANDS, stride=SLOT_ROWS), :]
    keep = notes[0:1, KEEP_LANE : KEEP_LANE + 1]
    target = lax.broadcasted_iota(jnp.int32, (BANDS, LOWS), 1).astype(F32)
    sources, hits = [], []
    for p in range(0, PAIRS, 2):
        couple = [flat[pl.ds(p + i, BANDS, stride=SLOT_ROWS), :] for i in range(2)]
        sources.append(jnp.concatenate(couple, axis=0).T.astype(BF16))
    for p in range(PAIRS):
        place = DIGIT * notes[:, p : p + 1] + notes[:, PAIRS + p : PAIRS + p + 1]
        hits.append(jnp.where(target == place, 1.0, 0.0).astype(BF16))
    by_wave = jnp.dot(
        jnp.concatenate(sources, axis=1),
        jnp.concatenate(hits, axis=0),
        preferred_element_type=F32,
    )
    for a in range(LOWS // BLK):
        sorted_buf[a] = by_wave[:, a * BLK : (a + 1) * BLK]
        for h in range(2):
            for c in range(2):
                for r in range(2):
                    series[2 * h + c, a, pl.ds(r, FIELDS, stride=2), :] = sorted_buf[
                        a, pl.ds(r * 64 + h * 32 + c, FIELDS, stride=2), :
                    ]
    first = lax.broadcasted_iota(jnp.int32, (2 * FIELDS, BLK), 1) < PER_CLASS
    table_copy.wait()
    real, imag = [], []
    for cls in range(RADIX):
        a = cls // 2
        b = RADIX // 2 - 1 - a
        halves = []
        for c in range(2):
            low = series[c, a]
            high = series[2 + c, b]
            halves.append(jnp.where(first, low, high) if cls % 2 == 0 else jnp.where(first, high, low))
        re, im = halves
        lhs = jnp.concatenate(
            [jnp.concatenate([re, im], axis=1), jnp.concatenate([im, -re], axis=1)], axis=0
        ).astype(BF16)
        both = jnp.dot(lhs, table[cls], preferred_element_type=F32)
        real.append(both[: 2 * FIELDS])
        imag.append(both[2 * FIELDS :])
    pieces = [None] * RADIX
    for q in range(3):
        sums = []
        for part, wave in ((real, math.cos), (imag, math.sin)):
            for odd in range(2):
                total = None
                for cls in range(odd, RADIX, 2):
                    factor = wave(2.0 * math.pi * cls * q / RADIX)
                    if abs(factor) < 1e-9:
                        continue
                    term = part[cls] if factor == 1.0 else part[cls] * factor
                    total = term if total is None else total + term
                sums.append(total)
        cos_even, cos_odd, sin_even, sin_odd = sums
        if q == 0:
            pieces[0] = cos_even + cos_odd
            pieces[5] = cos_even - cos_odd
        else:
            pieces[q] = (cos_even + cos_odd) - (sin_even + sin_odd)
            pieces[10 - q] = (cos_even + cos_odd) + (sin_even + sin_odd)
            pieces[5 - q] = (cos_even - cos_odd) + (sin_even - sin_odd)
            pieces[5 + q] = (cos_even - cos_odd) - (sin_even - sin_odd)
    second = lax.broadcasted_iota(jnp.int32, (2 * FIELDS, STEP), 0) % 2
    kept = keep > 0.5
    basis_copy.wait()
    total = jnp.zeros((2 * FIELDS, MODES), F32)
    for q in range(RADIX):
        window = slice(q * STEP, (q + 1) * STEP)
        upper_row = jnp.where(second == 0, pieces[q], 0.0)
        lower_row = jnp.where((second == 1) & kept, pieces[q], 0.0)
        grid_out[:, :, window] = (
            (upper_row + lower_row).astype(BF16).reshape(FIELDS, 2, STEP)
        )
        total += jnp.dot(upper_row.astype(BF16), basis[0, window, :], preferred_element_type=F32)
        total += jnp.dot(lower_row.astype(BF16), basis[1, window, :], preferred_element_type=F32)
    for i in range(MODES // BLK):
        partial_buf[i] = total[:, i * BLK : (i + 1) * BLK]
        turned[i * BLK : (i + 1) * BLK, :FIELDS] = (
            partial_buf[i, pl.ds(0, FIELDS, stride=2), :]
            + partial_buf[i, pl.ds(1, FIELDS, stride=2), :]
        ).T
    share_out[...] = jnp.concatenate(
        [turned[pl.ds(o, BANDS, stride=SHARE), :][:, :FIELDS] for o in range(SHARE)], axis=1
    )


def sum_kernel(shares, out):
    out[...] = jnp.broadcast_to(jnp.sum(shares[...], axis=0, keepdims=True), out.shape)


VMEM = pl.BlockSpec(memory_space=pltpu.VMEM)
SMEM = pl.BlockSpec(memory_space=pltpu.SMEM)
HBM = pl.BlockSpec(memory_space=pl.ANY)
PARAMS = pltpu.CompilerParams(vmem_limit_bytes=48 * 1024 * 1024)


def to_messages(waves, lengths, spectra, legendre):
    return pl.pallas_call(
        legendre_kernel,
        out_shape=jax.ShapeDtypeStruct((BANDS, SLOT_ROWS, BLK), BF16),
        in_specs=[SMEM, VMEM, HBM, HBM],
        out_specs=VMEM,
        scratch_shapes=[
            pltpu.VMEM((PAIRS, FIELDS, 2, PAIR_LEN), BF16),
            pltpu.VMEM((PAIRS, HALF, PAIR_LEN), BF16),
            pltpu.VMEM((BANDS * SLOT_ROWS, BLK), F32),
            pltpu.SemaphoreType.DMA((2, PAIRS)),
        ],
        compiler_params=PARAMS,
    )(waves, lengths, spectra, legendre)


def to_grid(arrived, table, basis):
    return pl.pallas_call(
        synthesis_kernel,
        out_shape=(
            jax.ShapeDtypeStruct((FIELDS, 2, LON), BF16),
            jax.ShapeDtypeStruct((BANDS, SHARE * FIELDS), F32),
        ),
        in_specs=[VMEM, HBM, HBM],
        out_specs=(VMEM, VMEM),
        scratch_shapes=[
            pltpu.VMEM((BANDS * SLOT_ROWS, BLK), F32),
            pltpu.VMEM((LOWS // BLK, BLK, BLK), F32),
            pltpu.VMEM((4, LOWS // BLK, 2 * FIELDS, BLK), F32),
            pltpu.VMEM((MODES // BLK, 2 * FIELDS, BLK), F32),
            pltpu.VMEM((MODES, BLK), F32),
            pltpu.VMEM((RADIX, STEP, STEP), BF16),
            pltpu.VMEM((2, LON, MODES), BF16),
            pltpu.SemaphoreType.DMA((2,)),
        ],
        compiler_params=PARAMS,
    )(arrived, table, basis)


def to_sums(shares, copies):
    return pl.pallas_call(
        sum_kernel,
        out_shape=jax.ShapeDtypeStruct((copies, SHARE * FIELDS), F32),
        in_specs=[VMEM],
        out_specs=VMEM,
    )(shares)


def shards(spectra, legendre, pair_waves, band_lengths, eof_basis):
    ens, fields, levels, parts, slots = spectra.shape
    messages = to_messages(
        pair_waves,
        band_lengths.reshape(1, BANDS),
        spectra.reshape(FIELDS, parts, slots),
        legendre,
    )
    arrived = lax.all_to_all(messages, "band", 0, 0, tiled=True)
    grid, shares = to_grid(arrived, jnp.asarray(wave_table()), eof_basis)
    shares = lax.all_to_all(shares, "band", 0, 0, tiled=True)
    groups = lax.axis_size("mem")
    sums = to_sums(shares, groups)
    everyone = lax.all_to_all(sums, "mem", 0, 0, tiled=True)
    own = sums[0].reshape(SHARE, ens, fields * levels)
    total = jnp.sum(everyone, axis=0).reshape(SHARE, ens, fields * levels)
    mean = jnp.sum(total, axis=1, keepdims=True) / (ens * groups)
    anomaly = (own - mean).transpose(1, 2, 0).reshape(ens, fields, levels, SHARE)
    return grid.reshape(ens, fields, levels, 2, LON), anomaly


def solution(mesh):
    return jax.shard_map(
        shards,
        mesh=mesh,
        in_specs=(
            P("mem", None, None, None, "band"),
            P(None, "band"),
            P("band"),
            P(),
            P("band", None, None),
        ),
        out_specs=(P("mem", None, None, "band", None), P("mem", None, None, "band")),
        check_vma=False,
    )
```

```python
import math

import jax
import jax.numpy as jnp
import numpy as np
from jax import lax
from jax.experimental import pallas as pl
from jax.experimental.pallas import tpu as pltpu
from jax.sharding import PartitionSpec as P

WAVE_COUNT = 1280
LON = 2560
BLK = 128
HALF = 40
BANDS = 64
PAIRS = 10
PAIR_LEN = 1408
FIELDS = 16
RADIX = 10
STEP = LON // RADIX
MODES = 256
SHARE = MODES // BANDS
SLOT_ROWS = 12
LOADS = 2
LOWS = WAVE_COUNT // 2
PER_CLASS = LOWS // RADIX
DIGIT = 16
KEEP_LANE = 2 * PAIRS
F32 = jnp.float32
BF16 = jnp.bfloat16


def wave_table():
    ladder = RADIX * np.arange(PER_CLASS)
    parts = []
    for c in range(RADIX):
        low = ladder + c
        high = WAVE_COUNT - RADIX - ladder + c
        orders = np.concatenate([low, high] if c % 2 == 0 else [high, low])
        phase = orders[:, None] * np.arange(STEP)[None, :] % LON
        angle = phase.astype(np.float32) * np.float32(2.0 * math.pi / LON)
        weight = np.where(orders == 0, 1.0, 2.0).astype(np.float32)[:, None]
        parts.append(np.concatenate([weight * np.cos(angle), -weight * np.sin(angle)]))
    return np.stack(parts).astype(jnp.bfloat16)


def legendre_kernel(
    waves_hbm, lengths_hbm, spectra_hbm, legendre_hbm, out,
    waves, lengths, spectra_buf, legendre_buf, flat, sems, small_sems,
):
    waves_copy = pltpu.make_async_copy(waves_hbm, waves, small_sems.at[0])
    lengths_copy = pltpu.make_async_copy(lengths_hbm, lengths, small_sems.at[1])
    waves_copy.start()
    lengths_copy.start()

    loads = []
    for i in range(LOADS):
        window = pl.ds(i * (PAIRS // LOADS) * PAIR_LEN, (PAIRS // LOADS) * PAIR_LEN)
        loads += [
            pltpu.make_async_copy(
                spectra_hbm.at[:, :, window], spectra_buf.at[:, :, window], sems.at[0, i]
            ),
            pltpu.make_async_copy(
                legendre_hbm.at[:, window], legendre_buf.at[:, window], sems.at[1, i]
            ),
        ]
    for load in loads:
        load.start()
    waves_copy.wait()
    lengths_copy.wait()
    counts = lengths[...].astype(F32)
    dest = lax.broadcasted_iota(jnp.int32, (BANDS, BANDS), 0)
    other = lax.broadcasted_iota(jnp.int32, (BANDS, BANDS), 1)
    starts = jnp.sum(jnp.where(other < dest, counts, 0.0), axis=1, keepdims=True)
    own = jnp.sum(jnp.where(other == dest, counts, 0.0), axis=1, keepdims=True)
    column = lax.broadcasted_iota(jnp.int32, (BANDS, 2 * HALF), 1).astype(F32)
    picks = []
    for r in range(2):
        row = jnp.minimum(starts + r, 2 * HALF - 1.0)
        source = jnp.where(row < HALF, row, 3 * HALF - 1.0 - row)
        picks.append((column == source).astype(BF16))
    pick = jnp.concatenate(picks, axis=0)
    lane = lax.broadcasted_iota(jnp.int32, (BANDS, BLK), 1)
    notes = jnp.where(lane == KEEP_LANE, jnp.where(own > 1.0, 1.0, 0.0), 0.0)
    position = lax.broadcasted_iota(jnp.int32, (FIELDS, PAIR_LEN), 1)
    parity = lax.broadcasted_iota(jnp.int32, (HALF, PAIR_LEN), 1) % 2
    alternate = jnp.where(parity == 0, 1.0, -1.0).astype(BF16)
    flat[...] = jnp.zeros(flat.shape, F32)
    for load in loads:
        load.wait()
    half = BLK // 2
    for p in range(PAIRS):
        wave = waves[p]
        place = (wave % RADIX) * PER_CLASS + wave // RADIX
        notes = jnp.where(lane == p, (place // DIGIT).astype(F32), notes)
        notes = jnp.where(lane == PAIRS + p, (place % DIGIT).astype(F32), notes)
        upper = position - (WAVE_COUNT // BLK - wave // BLK) * BLK
        low = (position < WAVE_COUNT - wave).astype(F32).astype(BF16)
        high = ((upper >= 0) & (upper < wave + 1)).astype(F32).astype(BF16)
        window = slice(p * PAIR_LEN, (p + 1) * PAIR_LEN)
        coeffs = spectra_buf[:, :, window].reshape(2 * FIELDS, PAIR_LEN)
        halves = [jnp.concatenate([mask, mask], axis=0) * coeffs for mask in (low, high)]
        masked = jnp.concatenate(halves, axis=0)
        north = legendre_buf[:, window]
        rows = jnp.concatenate([north, north * alternate], axis=0)
        fourier = lax.dot_general(
            rows, masked, (((1,), (1,)), ((), ())), preferred_element_type=F32
        )
        if p % 2 == 0:
            first = fourier
            continue
        couple = jnp.concatenate([first, fourier], axis=1).astype(BF16)
        picked = jnp.dot(pick, couple, preferred_element_type=F32)
        top, bottom = picked[:BANDS], picked[BANDS:]
        flat[pl.ds(p - 1, BANDS, stride=SLOT_ROWS), :] = jnp.concatenate(
            [top[:, :half], bottom[:, :half]], axis=1
        )
        flat[pl.ds(p, BANDS, stride=SLOT_ROWS), :] = jnp.concatenate(
            [top[:, half:], bottom[:, half:]], axis=1
        )
    flat[pl.ds(PAIRS, BANDS, stride=SLOT_ROWS), :] = notes
    out[...] = flat[...].astype(BF16)


def synthesis_kernel(
    arrived, table_hbm, basis, grid_out, share_out,
    flat, sorted_buf, series, partial_buf, turned, table, sems,
):
    loads = [
        pltpu.make_async_copy(
            table_hbm.at[pl.ds(i, 2)], table.at[pl.ds(i, 2)], sems.at[i // 2]
        )
        for i in range(0, RADIX, 2)
    ]
    for load in loads:
        load.start()
    flat[...] = arrived[...].astype(F32)
    notes = flat[pl.ds(PAIRS, BANDS, stride=SLOT_ROWS), :]
    keep = notes[0:1, KEEP_LANE : KEEP_LANE + 1]
    target = lax.broadcasted_iota(jnp.int32, (BANDS, LOWS), 1).astype(F32)
    sources, hits = [], []
    for p in range(0, PAIRS, 2):
        couple = [flat[pl.ds(p + i, BANDS, stride=SLOT_ROWS), :] for i in range(2)]
        sources.append(jnp.concatenate(couple, axis=0).T.astype(BF16))
    for p in range(PAIRS):
        place = DIGIT * notes[:, p : p + 1] + notes[:, PAIRS + p : PAIRS + p + 1]
        hits.append(jnp.where(target == place, 1.0, 0.0).astype(BF16))
    by_wave = jnp.dot(
        jnp.concatenate(sources, axis=1),
        jnp.concatenate(hits, axis=0),
        preferred_element_type=F32,
    )
    for a in range(LOWS // BLK):
        sorted_buf[a] = by_wave[:, a * BLK : (a + 1) * BLK]
        for h in range(2):
            for c in range(2):
                for r in range(2):
                    series[2 * h + c, a, pl.ds(r, FIELDS, stride=2), :] = sorted_buf[
                        a, pl.ds(r * 64 + h * 32 + c, FIELDS, stride=2), :
                    ]
    first = lax.broadcasted_iota(jnp.int32, (2 * FIELDS, BLK), 1) < PER_CLASS
    for load in loads:
        load.wait()
    real, imag = [], []
    for cls in range(RADIX):
        a = cls // 2
        b = RADIX // 2 - 1 - a
        halves = []
        for c in range(2):
            low = series[c, a]
            high = series[2 + c, b]
            halves.append(jnp.where(first, low, high) if cls % 2 == 0 else jnp.where(first, high, low))
        re, im = halves
        lhs = jnp.concatenate(
            [jnp.concatenate([re, im], axis=1), jnp.concatenate([im, -re], axis=1)], axis=0
        ).astype(BF16)
        both = jnp.dot(lhs, table[cls], preferred_element_type=F32)
        real.append(both[: 2 * FIELDS])
        imag.append(both[2 * FIELDS :])
    pieces = [None] * RADIX
    for q in range(3):
        sums = []
        for part, wave in ((real, math.cos), (imag, math.sin)):
            for odd in range(2):
                total = None
                for cls in range(odd, RADIX, 2):
                    factor = wave(2.0 * math.pi * cls * q / RADIX)
                    if abs(factor) < 1e-9:
                        continue
                    term = part[cls] if factor == 1.0 else part[cls] * factor
                    total = term if total is None else total + term
                sums.append(total)
        cos_even, cos_odd, sin_even, sin_odd = sums
        if q == 0:
            pieces[0] = cos_even + cos_odd
            pieces[5] = cos_even - cos_odd
        else:
            pieces[q] = (cos_even + cos_odd) - (sin_even + sin_odd)
            pieces[10 - q] = (cos_even + cos_odd) + (sin_even + sin_odd)
            pieces[5 - q] = (cos_even - cos_odd) + (sin_even - sin_odd)
            pieces[5 + q] = (cos_even - cos_odd) - (sin_even - sin_odd)
    second = lax.broadcasted_iota(jnp.int32, (2 * FIELDS, STEP), 0) % 2
    kept = keep > 0.5
    total = jnp.zeros((2 * FIELDS, MODES), F32)
    for q in range(RADIX):
        window = slice(q * STEP, (q + 1) * STEP)
        upper_row = jnp.where(second == 0, pieces[q], 0.0)
        lower_row = jnp.where((second == 1) & kept, pieces[q], 0.0)
        grid_out[:, :, window] = (
            (upper_row + lower_row).astype(BF16).reshape(FIELDS, 2, STEP)
        )
        total += jnp.dot(upper_row.astype(BF16), basis[0, window, :], preferred_element_type=F32)
        total += jnp.dot(lower_row.astype(BF16), basis[1, window, :], preferred_element_type=F32)
    for i in range(MODES // BLK):
        partial_buf[i] = total[:, i * BLK : (i + 1) * BLK]
        turned[i * BLK : (i + 1) * BLK, :FIELDS] = (
            partial_buf[i, pl.ds(0, FIELDS, stride=2), :]
            + partial_buf[i, pl.ds(1, FIELDS, stride=2), :]
        ).T
    share_out[...] = jnp.concatenate(
        [turned[pl.ds(o, BANDS, stride=SHARE), :][:, :FIELDS] for o in range(SHARE)], axis=1
    )


VMEM = pl.BlockSpec(memory_space=pltpu.VMEM)
HBM = pl.BlockSpec(memory_space=pltpu.HBM)
PARAMS = pltpu.CompilerParams(vmem_limit_bytes=48 * 1024 * 1024)


def to_messages(waves, lengths, spectra, legendre):
    return pl.pallas_call(
        legendre_kernel,
        out_shape=jax.ShapeDtypeStruct((BANDS * SLOT_ROWS, BLK), BF16),
        in_specs=[HBM, HBM, HBM, HBM],
        out_specs=VMEM,
        scratch_shapes=[
            pltpu.SMEM((PAIRS,), jnp.int32),
            pltpu.VMEM((1, BANDS), jnp.int32),
            pltpu.VMEM((FIELDS, 2, PAIRS * PAIR_LEN), BF16),
            pltpu.VMEM((HALF, PAIRS * PAIR_LEN), BF16),
            pltpu.VMEM((BANDS * SLOT_ROWS, BLK), F32),
            pltpu.SemaphoreType.DMA((2, LOADS)),
            pltpu.SemaphoreType.DMA((2,)),
        ],
        compiler_params=PARAMS,
    )(*[pltpu.with_memory_space_constraint(x, pltpu.HBM) for x in (waves, lengths, spectra, legendre)])


def to_grid(arrived, table, basis):
    return pl.pallas_call(
        synthesis_kernel,
        out_shape=(
            jax.ShapeDtypeStruct((FIELDS, 2, LON), BF16),
            jax.ShapeDtypeStruct((BANDS, SHARE * FIELDS), F32),
        ),
        in_specs=[VMEM, HBM, VMEM],
        out_specs=(VMEM, VMEM),
        scratch_shapes=[
            pltpu.VMEM((BANDS * SLOT_ROWS, BLK), F32),
            pltpu.VMEM((LOWS // BLK, BLK, BLK), F32),
            pltpu.VMEM((4, LOWS // BLK, 2 * FIELDS, BLK), F32),
            pltpu.VMEM((MODES // BLK, 2 * FIELDS, BLK), F32),
            pltpu.VMEM((MODES, BLK), F32),
            pltpu.VMEM((RADIX, STEP, STEP), BF16),
            pltpu.SemaphoreType.DMA((RADIX // 2,)),
        ],
        compiler_params=PARAMS,
    )(arrived, pltpu.with_memory_space_constraint(table, pltpu.HBM), basis)


def shards(spectra, legendre, pair_waves, band_lengths, eof_basis):
    ens, fields, levels, parts, slots = spectra.shape
    messages = to_messages(
        pair_waves,
        band_lengths.reshape(1, BANDS),
        spectra.reshape(FIELDS, parts, slots),
        legendre,
    )
    messages = messages.reshape(BANDS, SLOT_ROWS // 2, 2, BLK)
    arrived = lax.all_to_all(messages, "band", 0, 0, tiled=True)
    arrived = arrived.reshape(BANDS * SLOT_ROWS, BLK)
    grid, shares = to_grid(arrived, jnp.asarray(wave_table()), eof_basis)
    shares = lax.all_to_all(shares, "band", 0, 0, tiled=True)
    groups = lax.axis_size("mem")
    sums = jnp.broadcast_to(jnp.sum(shares, axis=0)[None], (groups, SHARE * FIELDS))
    everyone = lax.all_to_all(sums, "mem", 0, 0, tiled=True)
    own = sums[0].reshape(SHARE, ens, fields * levels)
    total = jnp.sum(everyone, axis=0).reshape(SHARE, ens, fields * levels)
    mean = jnp.sum(total, axis=1, keepdims=True) / (ens * groups)
    anomaly = (own - mean).transpose(1, 2, 0).reshape(ens, fields, levels, SHARE)
    return grid.reshape(ens, fields, levels, 2, LON), anomaly


def solution(mesh):
    return jax.shard_map(
        shards,
        mesh=mesh,
        in_specs=(
            P("mem", None, None, None, "band"),
            P(None, "band"),
            P("band"),
            P(),
            P("band", None, None),
        ),
        out_specs=(P("mem", None, None, "band", None), P("mem", None, None, "band")),
        check_vma=False,
    )
```

```python
import math

import jax
import jax.numpy as jnp
import numpy as np
from jax import lax
from jax.experimental import pallas as pl
from jax.experimental.pallas import tpu as pltpu
from jax.sharding import PartitionSpec as P

WAVE_COUNT = 1280
LON = 2560
BLK = 128
HALF = 40
BANDS = 64
PAIRS = 10
PAIR_LEN = 1408
FIELDS = 16
RADIX = 10
STEP = LON // RADIX
MODES = 256
SHARE = MODES // BANDS
SLOT_ROWS = 12
LOADS = 2
LOWS = WAVE_COUNT // 2
PER_CLASS = LOWS // RADIX
DIGIT = 16
KEEP_LANE = 2 * PAIRS
F32 = jnp.float32
BF16 = jnp.bfloat16


def wave_table():
    ladder = RADIX * np.arange(PER_CLASS)
    parts = []
    for c in range(RADIX):
        low = ladder + c
        high = WAVE_COUNT - RADIX - ladder + c
        orders = np.concatenate([low, high] if c % 2 == 0 else [high, low])
        phase = orders[:, None] * np.arange(STEP)[None, :] % LON
        angle = phase.astype(np.float32) * np.float32(2.0 * math.pi / LON)
        weight = np.where(orders == 0, 1.0, 2.0).astype(np.float32)[:, None]
        parts.append(np.concatenate([weight * np.cos(angle), -weight * np.sin(angle)]))
    return np.stack(parts).astype(jnp.bfloat16)


def legendre_kernel(
    waves_hbm, lengths_hbm, spectra_hbm, legendre_hbm, table_hbm, out, table,
    waves, lengths, spectra_buf, legendre_buf, flat, sems, small_sems,
):
    waves_copy = pltpu.make_async_copy(waves_hbm, waves, small_sems.at[0])
    lengths_copy = pltpu.make_async_copy(lengths_hbm, lengths, small_sems.at[1])
    waves_copy.start()
    lengths_copy.start()

    loads = []
    for i in range(LOADS):
        window = pl.ds(i * (PAIRS // LOADS) * PAIR_LEN, (PAIRS // LOADS) * PAIR_LEN)
        loads += [
            pltpu.make_async_copy(
                spectra_hbm.at[:, :, window], spectra_buf.at[:, :, window], sems.at[0, i]
            ),
            pltpu.make_async_copy(
                legendre_hbm.at[:, window], legendre_buf.at[:, window], sems.at[1, i]
            ),
        ]
    for load in loads:
        load.start()
    table_copy = pltpu.make_async_copy(table_hbm, table, small_sems.at[2])
    table_copy.start()
    waves_copy.wait()
    lengths_copy.wait()
    counts = lengths[...].astype(F32)
    dest = lax.broadcasted_iota(jnp.int32, (BANDS, BANDS), 0)
    other = lax.broadcasted_iota(jnp.int32, (BANDS, BANDS), 1)
    starts = jnp.sum(jnp.where(other < dest, counts, 0.0), axis=1, keepdims=True)
    own = jnp.sum(jnp.where(other == dest, counts, 0.0), axis=1, keepdims=True)
    column = lax.broadcasted_iota(jnp.int32, (BANDS, 2 * HALF), 1).astype(F32)
    picks = []
    for r in range(2):
        row = jnp.minimum(starts + r, 2 * HALF - 1.0)
        source = jnp.where(row < HALF, row, 3 * HALF - 1.0 - row)
        picks.append((column == source).astype(BF16))
    pick = jnp.concatenate(picks, axis=0)
    lane = lax.broadcasted_iota(jnp.int32, (BANDS, BLK), 1)
    notes = jnp.where(lane == KEEP_LANE, jnp.where(own > 1.0, 1.0, 0.0), 0.0)
    position = lax.broadcasted_iota(jnp.int32, (FIELDS, PAIR_LEN), 1)
    parity = lax.broadcasted_iota(jnp.int32, (HALF, PAIR_LEN), 1) % 2
    alternate = jnp.where(parity == 0, 1.0, -1.0).astype(BF16)
    flat[...] = jnp.zeros(flat.shape, F32)
    for load in loads:
        load.wait()
    half = BLK // 2
    for p in range(PAIRS):
        wave = waves[p]
        place = (wave % RADIX) * PER_CLASS + wave // RADIX
        notes = jnp.where(lane == p, (place // DIGIT).astype(F32), notes)
        notes = jnp.where(lane == PAIRS + p, (place % DIGIT).astype(F32), notes)
        upper = position - (WAVE_COUNT // BLK - wave // BLK) * BLK
        low = (position < WAVE_COUNT - wave).astype(F32).astype(BF16)
        high = ((upper >= 0) & (upper < wave + 1)).astype(F32).astype(BF16)
        window = slice(p * PAIR_LEN, (p + 1) * PAIR_LEN)
        coeffs = spectra_buf[:, :, window].reshape(2 * FIELDS, PAIR_LEN)
        halves = [jnp.concatenate([mask, mask], axis=0) * coeffs for mask in (low, high)]
        masked = jnp.concatenate(halves, axis=0)
        north = legendre_buf[:, window]
        rows = jnp.concatenate([north, north * alternate], axis=0)
        fourier = lax.dot_general(
            masked, rows, (((1,), (1,)), ((), ())), preferred_element_type=F32
        )
        every = ([] if p == 0 else every) + [fourier]
        if p < PAIRS - 1:
            continue
        couple = jnp.concatenate(every, axis=0).astype(BF16)
        picked = lax.dot_general(
            pick, couple, (((1,), (1,)), ((), ())), preferred_element_type=F32
        )
        top, bottom = picked[:BANDS], picked[BANDS:]
        for i in range(PAIRS):
            flat[pl.ds(i, BANDS, stride=SLOT_ROWS), :] = jnp.concatenate(
                [top[:, i * half : (i + 1) * half], bottom[:, i * half : (i + 1) * half]], axis=1
            )
    flat[pl.ds(PAIRS, BANDS, stride=SLOT_ROWS), :] = notes
    out[...] = flat[...].astype(BF16)
    table_copy.wait()


def synthesis_kernel(
    arrived, table, basis, grid_out, share_out,
    flat, sorted_buf, series, partial_buf, turned,
):
    flat[...] = arrived[...].astype(F32)
    notes = flat[pl.ds(PAIRS, BANDS, stride=SLOT_ROWS), :]
    keep = notes[0:1, KEEP_LANE : KEEP_LANE + 1]
    target = lax.broadcasted_iota(jnp.int32, (BANDS, LOWS), 1).astype(F32)
    sources, hits = [], []
    for p in range(0, PAIRS, 2):
        couple = [flat[pl.ds(p + i, BANDS, stride=SLOT_ROWS), :] for i in range(2)]
        sources.append(jnp.concatenate(couple, axis=0).T.astype(BF16))
    for p in range(PAIRS):
        place = DIGIT * notes[:, p : p + 1] + notes[:, PAIRS + p : PAIRS + p + 1]
        hits.append(jnp.where(target == place, 1.0, 0.0).astype(BF16))
    by_wave = jnp.dot(
        jnp.concatenate(sources, axis=1),
        jnp.concatenate(hits, axis=0),
        preferred_element_type=F32,
    )
    for a in range(LOWS // BLK):
        sorted_buf[a] = by_wave[:, a * BLK : (a + 1) * BLK]
        for h in range(2):
            for c in range(2):
                for r in range(2):
                    series[2 * h + c, a, pl.ds(r, FIELDS, stride=2), :] = sorted_buf[
                        a, pl.ds(r * 64 + h * 32 + c, FIELDS, stride=2), :
                    ]
    first = lax.broadcasted_iota(jnp.int32, (2 * FIELDS, BLK), 1) < PER_CLASS
    real, imag = [], []
    for cls in range(RADIX):
        a = cls // 2
        b = RADIX // 2 - 1 - a
        halves = []
        for c in range(2):
            low = series[c, a]
            high = series[2 + c, b]
            halves.append(jnp.where(first, low, high) if cls % 2 == 0 else jnp.where(first, high, low))
        re, im = halves
        lhs = jnp.concatenate(
            [jnp.concatenate([re, im], axis=1), jnp.concatenate([im, -re], axis=1)], axis=0
        ).astype(BF16)
        both = jnp.dot(lhs, table[cls], preferred_element_type=F32)
        real.append(both[: 2 * FIELDS])
        imag.append(both[2 * FIELDS :])
    pieces = [None] * RADIX
    for q in range(3):
        sums = []
        for part, wave in ((real, math.cos), (imag, math.sin)):
            for odd in range(2):
                total = None
                for cls in range(odd, RADIX, 2):
                    factor = wave(2.0 * math.pi * cls * q / RADIX)
                    if abs(factor) < 1e-9:
                        continue
                    term = part[cls] if factor == 1.0 else part[cls] * factor
                    total = term if total is None else total + term
                sums.append(total)
        cos_even, cos_odd, sin_even, sin_odd = sums
        if q == 0:
            pieces[0] = cos_even + cos_odd
            pieces[5] = cos_even - cos_odd
        else:
            pieces[q] = (cos_even + cos_odd) - (sin_even + sin_odd)
            pieces[10 - q] = (cos_even + cos_odd) + (sin_even + sin_odd)
            pieces[5 - q] = (cos_even - cos_odd) + (sin_even - sin_odd)
            pieces[5 + q] = (cos_even - cos_odd) - (sin_even - sin_odd)
    second = lax.broadcasted_iota(jnp.int32, (2 * FIELDS, STEP), 0) % 2
    kept = keep > 0.5
    uppers, lowers = [], []
    for q in range(RADIX):
        upper_row = jnp.where(second == 0, pieces[q], 0.0)
        lower_row = jnp.where((second == 1) & kept, pieces[q], 0.0)
        grid_out[:, :, q * STEP : (q + 1) * STEP] = (
            (upper_row + lower_row).astype(BF16).reshape(FIELDS, 2, STEP)
        )
        uppers.append(upper_row.astype(BF16))
        lowers.append(lower_row.astype(BF16))
    total = jnp.dot(
        jnp.concatenate(uppers + lowers, axis=1),
        basis[...].reshape(2 * LON, MODES),
        preferred_element_type=F32,
    )
    for i in range(MODES // BLK):
        partial_buf[i] = total[:, i * BLK : (i + 1) * BLK]
        turned[i * BLK : (i + 1) * BLK, :FIELDS] = (
            partial_buf[i, pl.ds(0, FIELDS, stride=2), :]
            + partial_buf[i, pl.ds(1, FIELDS, stride=2), :]
        ).T
    share_out[...] = jnp.concatenate(
        [turned[pl.ds(o, BANDS, stride=SHARE), :][:, :FIELDS] for o in range(SHARE)], axis=1
    )


VMEM = pl.BlockSpec(memory_space=pltpu.VMEM)
HBM = pl.BlockSpec(memory_space=pltpu.HBM)
PARAMS = pltpu.CompilerParams(vmem_limit_bytes=48 * 1024 * 1024)


def to_messages(waves, lengths, spectra, legendre, table):
    return pl.pallas_call(
        legendre_kernel,
        out_shape=(
            jax.ShapeDtypeStruct((BANDS * SLOT_ROWS, BLK), BF16),
            jax.ShapeDtypeStruct((RADIX, STEP, STEP), BF16),
        ),
        in_specs=[HBM, HBM, HBM, HBM, HBM],
        out_specs=(VMEM, VMEM),
        scratch_shapes=[
            pltpu.SMEM((PAIRS,), jnp.int32),
            pltpu.VMEM((1, BANDS), jnp.int32),
            pltpu.VMEM((FIELDS, 2, PAIRS * PAIR_LEN), BF16),
            pltpu.VMEM((HALF, PAIRS * PAIR_LEN), BF16),
            pltpu.VMEM((BANDS * SLOT_ROWS, BLK), F32),
            pltpu.SemaphoreType.DMA((2, LOADS)),
            pltpu.SemaphoreType.DMA((3,)),
        ],
        compiler_params=PARAMS,
    )(*[pltpu.with_memory_space_constraint(x, pltpu.HBM) for x in (waves, lengths, spectra, legendre, table)])


def to_grid(arrived, table, basis):
    return pl.pallas_call(
        synthesis_kernel,
        out_shape=(
            jax.ShapeDtypeStruct((FIELDS, 2, LON), BF16),
            jax.ShapeDtypeStruct((BANDS, SHARE * FIELDS), F32),
        ),
        in_specs=[VMEM, VMEM, VMEM],
        out_specs=(VMEM, VMEM),
        scratch_shapes=[
            pltpu.VMEM((BANDS * SLOT_ROWS, BLK), F32),
            pltpu.VMEM((LOWS // BLK, BLK, BLK), F32),
            pltpu.VMEM((4, LOWS // BLK, 2 * FIELDS, BLK), F32),
            pltpu.VMEM((MODES // BLK, 2 * FIELDS, BLK), F32),
            pltpu.VMEM((MODES, BLK), F32),
        ],
        compiler_params=PARAMS,
    )(arrived, table, basis)


def shards(spectra, legendre, pair_waves, band_lengths, eof_basis):
    ens, fields, levels, parts, slots = spectra.shape
    messages, table = to_messages(
        pair_waves,
        band_lengths.reshape(1, BANDS),
        spectra.reshape(FIELDS, parts, slots),
        legendre,
        jnp.asarray(wave_table()),
    )
    messages = messages.reshape(BANDS, SLOT_ROWS // 2, 2, BLK)
    arrived = lax.all_to_all(messages, "band", 0, 0, tiled=True)
    arrived = arrived.reshape(BANDS * SLOT_ROWS, BLK)
    grid, shares = to_grid(arrived, table, eof_basis)
    shares = lax.all_to_all(shares, "band", 0, 0, tiled=True)
    groups = lax.axis_size("mem")
    sums = jnp.broadcast_to(jnp.sum(shares, axis=0)[None], (groups, SHARE * FIELDS))
    everyone = lax.all_to_all(sums, "mem", 0, 0, tiled=True)
    everyone, sums = lax.optimization_barrier((everyone, sums))
    own = sums[0].reshape(SHARE, ens, fields * levels)
    total = jnp.sum(everyone, axis=0).reshape(SHARE, ens, fields * levels)
    mean = jnp.sum(total, axis=1, keepdims=True) / (ens * groups)
    anomaly = (own - mean).transpose(1, 2, 0).reshape(ens, fields, levels, SHARE)
    return grid.reshape(ens, fields, levels, 2, LON), anomaly


def solution(mesh):
    return jax.shard_map(
        shards,
        mesh=mesh,
        in_specs=(
            P("mem", None, None, None, "band"),
            P(None, "band"),
            P("band"),
            P(),
            P("band", None, None),
        ),
        out_specs=(P("mem", None, None, "band", None), P("mem", None, None, "band")),
        check_vma=False,
    )
```

```python
import math

import jax
import jax.numpy as jnp
import numpy as np
from jax import lax
from jax.experimental import pallas as pl
from jax.experimental.pallas import tpu as pltpu
from jax.sharding import PartitionSpec as P

WAVE_COUNT = 1280
LON = 2560
BLK = 128
HALF = 40
BANDS = 64
PAIRS = 10
PAIR_LEN = 1408
FIELDS = 16
RADIX = 10
STEP = LON // RADIX
MODES = 256
SHARE = MODES // BANDS
SLOT_ROWS = 12
LOADS = 2
LOWS = WAVE_COUNT // 2
PER_CLASS = LOWS // RADIX
DIGIT = 16
KEEP_LANE = 2 * PAIRS
F32 = jnp.float32
BF16 = jnp.bfloat16


def wave_table():
    ladder = RADIX * np.arange(PER_CLASS)
    parts = []
    for c in range(RADIX):
        low = ladder + c
        high = WAVE_COUNT - RADIX - ladder + c
        orders = np.concatenate([low, high] if c % 2 == 0 else [high, low])
        phase = orders[:, None] * np.arange(STEP)[None, :] % LON
        angle = phase.astype(np.float32) * np.float32(2.0 * math.pi / LON)
        weight = np.where(orders == 0, 1.0, 2.0).astype(np.float32)[:, None]
        parts.append(np.concatenate([weight * np.cos(angle), -weight * np.sin(angle)]))
    return np.stack(parts).astype(jnp.bfloat16)


def legendre_kernel(
    waves_hbm, lengths_hbm, spectra_hbm, legendre_hbm, table_hbm, out, table,
    waves, lengths, spectra_buf, legendre_buf, flat, sems, small_sems,
):
    waves_copy = pltpu.make_async_copy(waves_hbm, waves, small_sems.at[0])
    lengths_copy = pltpu.make_async_copy(lengths_hbm, lengths, small_sems.at[1])
    waves_copy.start()
    lengths_copy.start()

    loads = []
    for i in range(LOADS):
        window = pl.ds(i * (PAIRS // LOADS) * PAIR_LEN, (PAIRS // LOADS) * PAIR_LEN)
        loads += [
            pltpu.make_async_copy(
                spectra_hbm.at[:, :, window], spectra_buf.at[:, :, window], sems.at[0, i]
            ),
            pltpu.make_async_copy(
                legendre_hbm.at[:, window], legendre_buf.at[:, window], sems.at[1, i]
            ),
        ]
    for load in loads:
        load.start()
    table_copy = pltpu.make_async_copy(table_hbm, table, small_sems.at[2])
    table_copy.start()
    waves_copy.wait()
    lengths_copy.wait()
    counts = lengths[...].astype(F32)
    dest = lax.broadcasted_iota(jnp.int32, (BANDS, BANDS), 0)
    other = lax.broadcasted_iota(jnp.int32, (BANDS, BANDS), 1)
    starts = jnp.sum(jnp.where(other < dest, counts, 0.0), axis=1, keepdims=True)
    own = jnp.sum(jnp.where(other == dest, counts, 0.0), axis=1, keepdims=True)
    column = lax.broadcasted_iota(jnp.int32, (BANDS, 2 * HALF), 1).astype(F32)
    picks = []
    for r in range(2):
        row = jnp.minimum(starts + r, 2 * HALF - 1.0)
        source = jnp.where(row < HALF, row, 3 * HALF - 1.0 - row)
        picks.append((column == source).astype(BF16))
    pick = jnp.concatenate(picks, axis=0)
    lane = lax.broadcasted_iota(jnp.int32, (BANDS, BLK), 1)
    notes = jnp.where(lane == KEEP_LANE, jnp.where(own > 1.0, 1.0, 0.0), 0.0)
    position = lax.broadcasted_iota(jnp.int32, (FIELDS, PAIR_LEN), 1)
    parity = lax.broadcasted_iota(jnp.int32, (HALF, PAIR_LEN), 1) % 2
    alternate = jnp.where(parity == 0, 1.0, -1.0).astype(BF16)
    flat[...] = jnp.zeros(flat.shape, F32)
    half = BLK // 2
    for p in range(PAIRS):
        if p % (PAIRS // LOADS) == 0:
            for load in loads[2 * p * LOADS // PAIRS :][:2]:
                load.wait()
        wave = waves[p]
        place = (wave % RADIX) * PER_CLASS + wave // RADIX
        notes = jnp.where(lane == p, (place // DIGIT).astype(F32), notes)
        notes = jnp.where(lane == PAIRS + p, (place % DIGIT).astype(F32), notes)
        upper = position - (WAVE_COUNT // BLK - wave // BLK) * BLK
        low = (position < WAVE_COUNT - wave).astype(F32).astype(BF16)
        high = ((upper >= 0) & (upper < wave + 1)).astype(F32).astype(BF16)
        window = slice(p * PAIR_LEN, (p + 1) * PAIR_LEN)
        coeffs = spectra_buf[:, :, window].reshape(2 * FIELDS, PAIR_LEN)
        halves = [jnp.concatenate([mask, mask], axis=0) * coeffs for mask in (low, high)]
        masked = jnp.concatenate(halves, axis=0)
        north = legendre_buf[:, window]
        rows = jnp.concatenate([north, north * alternate], axis=0)
        fourier = lax.dot_general(
            masked, rows, (((1,), (1,)), ((), ())), preferred_element_type=F32
        )
        every = ([] if p == 0 else every) + [fourier]
        if p < PAIRS - 1:
            continue
        couple = jnp.concatenate(every, axis=0).astype(BF16)
        picked = lax.dot_general(
            pick, couple, (((1,), (1,)), ((), ())), preferred_element_type=F32
        )
        top, bottom = picked[:BANDS], picked[BANDS:]
        for i in range(PAIRS):
            flat[pl.ds(i, BANDS, stride=SLOT_ROWS), :] = jnp.concatenate(
                [top[:, i * half : (i + 1) * half], bottom[:, i * half : (i + 1) * half]], axis=1
            )
    flat[pl.ds(PAIRS, BANDS, stride=SLOT_ROWS), :] = notes
    out[...] = flat[...].astype(BF16)
    table_copy.wait()


def synthesis_kernel(
    arrived, table, basis, grid_out, share_out,
    flat, sorted_buf, series, partial_buf, turned,
):
    flat[...] = arrived[...].astype(F32)
    notes = flat[pl.ds(PAIRS, BANDS, stride=SLOT_ROWS), :]
    keep = notes[0:1, KEEP_LANE : KEEP_LANE + 1]
    target = lax.broadcasted_iota(jnp.int32, (BANDS, LOWS), 1).astype(F32)
    sources, hits = [], []
    for p in range(0, PAIRS, 2):
        couple = [flat[pl.ds(p + i, BANDS, stride=SLOT_ROWS), :] for i in range(2)]
        sources.append(jnp.concatenate(couple, axis=0).T.astype(BF16))
    for p in range(PAIRS):
        place = DIGIT * notes[:, p : p + 1] + notes[:, PAIRS + p : PAIRS + p + 1]
        hits.append(jnp.where(target == place, 1.0, 0.0).astype(BF16))
    by_wave = jnp.dot(
        jnp.concatenate(sources, axis=1),
        jnp.concatenate(hits, axis=0),
        preferred_element_type=F32,
    )
    for a in range(LOWS // BLK):
        sorted_buf[a] = by_wave[:, a * BLK : (a + 1) * BLK]
        for h in range(2):
            for c in range(2):
                for r in range(2):
                    series[2 * h + c, a, pl.ds(r, FIELDS, stride=2), :] = sorted_buf[
                        a, pl.ds(r * 64 + h * 32 + c, FIELDS, stride=2), :
                    ]
    first = lax.broadcasted_iota(jnp.int32, (2 * FIELDS, BLK), 1) < PER_CLASS
    real, imag = [], []
    for cls in range(RADIX):
        a = cls // 2
        b = RADIX // 2 - 1 - a
        halves = []
        for c in range(2):
            low = series[c, a]
            high = series[2 + c, b]
            halves.append(jnp.where(first, low, high) if cls % 2 == 0 else jnp.where(first, high, low))
        re, im = halves
        lhs = jnp.concatenate(
            [jnp.concatenate([re, im], axis=1), jnp.concatenate([im, -re], axis=1)], axis=0
        ).astype(BF16)
        both = jnp.dot(lhs, table[cls], preferred_element_type=F32)
        real.append(both[: 2 * FIELDS])
        imag.append(both[2 * FIELDS :])
    pieces = [None] * RADIX
    for q in range(3):
        sums = []
        for part, wave in ((real, math.cos), (imag, math.sin)):
            for odd in range(2):
                total = None
                for cls in range(odd, RADIX, 2):
                    factor = wave(2.0 * math.pi * cls * q / RADIX)
                    if abs(factor) < 1e-9:
                        continue
                    term = part[cls] if factor == 1.0 else part[cls] * factor
                    total = term if total is None else total + term
                sums.append(total)
        cos_even, cos_odd, sin_even, sin_odd = sums
        if q == 0:
            pieces[0] = cos_even + cos_odd
            pieces[5] = cos_even - cos_odd
        else:
            pieces[q] = (cos_even + cos_odd) - (sin_even + sin_odd)
            pieces[10 - q] = (cos_even + cos_odd) + (sin_even + sin_odd)
            pieces[5 - q] = (cos_even - cos_odd) + (sin_even - sin_odd)
            pieces[5 + q] = (cos_even - cos_odd) - (sin_even - sin_odd)
    second = lax.broadcasted_iota(jnp.int32, (2 * FIELDS, STEP), 0) % 2
    kept = keep > 0.5
    uppers, lowers = [], []
    for q in range(RADIX):
        upper_row = jnp.where(second == 0, pieces[q], 0.0)
        lower_row = jnp.where((second == 1) & kept, pieces[q], 0.0)
        grid_out[:, :, q * STEP : (q + 1) * STEP] = (
            (upper_row + lower_row).astype(BF16).reshape(FIELDS, 2, STEP)
        )
        uppers.append(upper_row.astype(BF16))
        lowers.append(lower_row.astype(BF16))
    lhs = jnp.concatenate(uppers + lowers, axis=1)
    rhs = basis[...].reshape(2 * LON, MODES)
    total = jnp.concatenate([jnp.dot(lhs, rhs[:, i*128:(i+1)*128], preferred_element_type=F32) for i in range(2)], axis=1)
    for i in range(MODES // BLK):
        partial_buf[i] = total[:, i * BLK : (i + 1) * BLK]
        turned[i * BLK : (i + 1) * BLK, :FIELDS] = (
            partial_buf[i, pl.ds(0, FIELDS, stride=2), :]
            + partial_buf[i, pl.ds(1, FIELDS, stride=2), :]
        ).T
    share_out[...] = jnp.concatenate(
        [turned[pl.ds(o, BANDS, stride=SHARE), :][:, :FIELDS] for o in range(SHARE)], axis=1
    )


VMEM = pl.BlockSpec(memory_space=pltpu.VMEM)
HBM = pl.BlockSpec(memory_space=pltpu.HBM)
PARAMS = pltpu.CompilerParams(vmem_limit_bytes=48 * 1024 * 1024)


def to_messages(waves, lengths, spectra, legendre, table):
    return pl.pallas_call(
        legendre_kernel,
        out_shape=(
            jax.ShapeDtypeStruct((BANDS * SLOT_ROWS, BLK), BF16),
            jax.ShapeDtypeStruct((RADIX, STEP, STEP), BF16),
        ),
        in_specs=[HBM, HBM, HBM, HBM, HBM],
        out_specs=(VMEM, VMEM),
        scratch_shapes=[
            pltpu.SMEM((PAIRS,), jnp.int32),
            pltpu.VMEM((1, BANDS), jnp.int32),
            pltpu.VMEM((FIELDS, 2, PAIRS * PAIR_LEN), BF16),
            pltpu.VMEM((HALF, PAIRS * PAIR_LEN), BF16),
            pltpu.VMEM((BANDS * SLOT_ROWS, BLK), F32),
            pltpu.SemaphoreType.DMA((2, LOADS)),
            pltpu.SemaphoreType.DMA((3,)),
        ],
        compiler_params=PARAMS,
    )(*[pltpu.with_memory_space_constraint(x, pltpu.HBM) for x in (waves, lengths, spectra, legendre, table)])


def to_grid(arrived, table, basis):
    return pl.pallas_call(
        synthesis_kernel,
        out_shape=(
            jax.ShapeDtypeStruct((FIELDS, 2, LON), BF16),
            jax.ShapeDtypeStruct((BANDS, SHARE * FIELDS), F32),
        ),
        in_specs=[VMEM, VMEM, VMEM],
        out_specs=(VMEM, VMEM),
        scratch_shapes=[
            pltpu.VMEM((BANDS * SLOT_ROWS, BLK), F32),
            pltpu.VMEM((LOWS // BLK, BLK, BLK), F32),
            pltpu.VMEM((4, LOWS // BLK, 2 * FIELDS, BLK), F32),
            pltpu.VMEM((MODES // BLK, 2 * FIELDS, BLK), F32),
            pltpu.VMEM((MODES, BLK), F32),
        ],
        compiler_params=PARAMS,
    )(arrived, table, basis)


def shards(spectra, legendre, pair_waves, band_lengths, eof_basis):
    ens, fields, levels, parts, slots = spectra.shape
    messages, table = to_messages(
        pair_waves,
        band_lengths.reshape(1, BANDS),
        spectra.reshape(FIELDS, parts, slots),
        legendre,
        jnp.asarray(wave_table()),
    )
    messages = messages.reshape(BANDS, SLOT_ROWS // 2, 2, BLK)
    arrived = lax.all_to_all(messages, "band", 0, 0, tiled=True)
    arrived = arrived.reshape(BANDS * SLOT_ROWS, BLK)
    grid, shares = to_grid(arrived, table, eof_basis)
    shares = lax.all_to_all(shares, "band", 0, 0, tiled=True)
    groups = lax.axis_size("mem")
    sums = jnp.broadcast_to(jnp.sum(shares, axis=0)[None], (groups, SHARE * FIELDS))
    everyone = lax.all_to_all(sums, "mem", 0, 0, tiled=True)
    everyone, sums = lax.optimization_barrier((everyone, sums))
    own = sums[0].reshape(SHARE, ens, fields * levels)
    total = jnp.sum(everyone, axis=0).reshape(SHARE, ens, fields * levels)
    mean = jnp.sum(total, axis=1, keepdims=True) / (ens * groups)
    anomaly = (own - mean).transpose(1, 2, 0).reshape(ens, fields, levels, SHARE)
    return grid.reshape(ens, fields, levels, 2, LON), anomaly


def solution(mesh):
    return jax.shard_map(
        shards,
        mesh=mesh,
        in_specs=(
            P("mem", None, None, None, "band"),
            P(None, "band"),
            P("band"),
            P(),
            P("band", None, None),
        ),
        out_specs=(P("mem", None, None, "band", None), P("mem", None, None, "band")),
        check_vma=False,
    )
```

```python
import math

import jax
import jax.numpy as jnp
import numpy as np
from jax import lax
from jax.experimental import pallas as pl
from jax.experimental.pallas import tpu as pltpu
from jax.sharding import Mesh
from jax.sharding import PartitionSpec as P

WAVE_COUNT = 1280
LON = 2560
BLK = 128
HALF = 40
BANDS = 64
RING = 8
PAIRS = 10
PAIR_LEN = 1408
FIELDS = 16
RADIX = 10
STEP = LON // RADIX
MODES = 256
SHARE = MODES // BANDS
SLOT_ROWS = 12
LOADS = 2
LOWS = WAVE_COUNT // 2
PER_CLASS = LOWS // RADIX
DIGIT = 16
KEEP_LANE = 2 * PAIRS
F32 = jnp.float32
BF16 = jnp.bfloat16


def wave_table():
    ladder = RADIX * np.arange(PER_CLASS)
    parts = []
    for c in range(RADIX):
        low = ladder + c
        high = WAVE_COUNT - RADIX - ladder + c
        orders = np.concatenate([low, high] if c % 2 == 0 else [high, low])
        phase = orders[:, None] * np.arange(STEP)[None, :] % LON
        angle = phase.astype(np.float32) * np.float32(2.0 * math.pi / LON)
        weight = np.where(orders == 0, 1.0, 2.0).astype(np.float32)[:, None]
        parts.append(np.concatenate([weight * np.cos(angle), -weight * np.sin(angle)]))
    return np.stack(parts).astype(jnp.bfloat16)


def legendre_kernel(
    waves_hbm, lengths_hbm, spectra_hbm, legendre_hbm, table_hbm, out, table,
    waves, lengths, spectra_buf, legendre_buf, flat, sems, small_sems,
):
    waves_copy = pltpu.make_async_copy(waves_hbm, waves, small_sems.at[0])
    lengths_copy = pltpu.make_async_copy(lengths_hbm, lengths, small_sems.at[1])
    waves_copy.start()
    lengths_copy.start()

    loads = []
    for i in range(LOADS):
        window = pl.ds(i * (PAIRS // LOADS) * PAIR_LEN, (PAIRS // LOADS) * PAIR_LEN)
        loads += [
            pltpu.make_async_copy(
                spectra_hbm.at[:, :, window], spectra_buf.at[:, :, window], sems.at[0, i]
            ),
            pltpu.make_async_copy(
                legendre_hbm.at[:, window], legendre_buf.at[:, window], sems.at[1, i]
            ),
        ]
    for load in loads:
        load.start()
    table_copy = pltpu.make_async_copy(table_hbm, table, small_sems.at[2])
    table_copy.start()
    waves_copy.wait()
    lengths_copy.wait()
    counts = lengths[...].astype(F32)
    order = lax.broadcasted_iota(jnp.int32, (BANDS, BANDS), 0)
    dest = (order % RING) * (BANDS // RING) + order // RING
    other = lax.broadcasted_iota(jnp.int32, (BANDS, BANDS), 1)
    starts = jnp.sum(jnp.where(other < dest, counts, 0.0), axis=1, keepdims=True)
    own = jnp.sum(jnp.where(other == dest, counts, 0.0), axis=1, keepdims=True)
    column = lax.broadcasted_iota(jnp.int32, (BANDS, 2 * HALF), 1).astype(F32)
    picks = []
    for r in range(2):
        row = jnp.minimum(starts + r, 2 * HALF - 1.0)
        source = jnp.where(row < HALF, row, 3 * HALF - 1.0 - row)
        picks.append((column == source).astype(BF16))
    pick = jnp.concatenate(picks, axis=0)
    lane = lax.broadcasted_iota(jnp.int32, (BANDS, BLK), 1)
    notes = jnp.where(lane == KEEP_LANE, jnp.where(own > 1.0, 1.0, 0.0), 0.0)
    position = lax.broadcasted_iota(jnp.int32, (FIELDS, PAIR_LEN), 1)
    parity = lax.broadcasted_iota(jnp.int32, (HALF, PAIR_LEN), 1) % 2
    alternate = jnp.where(parity == 0, 1.0, -1.0).astype(BF16)
    flat[...] = jnp.zeros(flat.shape, F32)
    half = BLK // 2
    for p in range(PAIRS):
        if p % (PAIRS // LOADS) == 0:
            for load in loads[2 * p * LOADS // PAIRS :][:2]:
                load.wait()
        wave = waves[p]
        place = (wave % RADIX) * PER_CLASS + wave // RADIX
        notes = jnp.where(lane == p, (place // DIGIT).astype(F32), notes)
        notes = jnp.where(lane == PAIRS + p, (place % DIGIT).astype(F32), notes)
        upper = position - (WAVE_COUNT // BLK - wave // BLK) * BLK
        low = (position < WAVE_COUNT - wave).astype(F32).astype(BF16)
        high = ((upper >= 0) & (upper < wave + 1)).astype(F32).astype(BF16)
        window = slice(p * PAIR_LEN, (p + 1) * PAIR_LEN)
        coeffs = spectra_buf[:, :, window].reshape(2 * FIELDS, PAIR_LEN)
        halves = [jnp.concatenate([mask, mask], axis=0) * coeffs for mask in (low, high)]
        masked = jnp.concatenate(halves, axis=0)
        north = legendre_buf[:, window]
        rows = jnp.concatenate([north, north * alternate], axis=0)
        fourier = lax.dot_general(
            masked, rows, (((1,), (1,)), ((), ())), preferred_element_type=F32
        )
        every = ([] if p == 0 else every) + [fourier]
        if p < PAIRS - 1:
            continue
        couple = jnp.concatenate(every, axis=0).astype(BF16)
        picked = lax.dot_general(
            pick, couple, (((1,), (1,)), ((), ())), preferred_element_type=F32
        )
        top, bottom = picked[:BANDS], picked[BANDS:]
        for i in range(PAIRS):
            flat[pl.ds(i, BANDS, stride=SLOT_ROWS), :] = jnp.concatenate(
                [top[:, i * half : (i + 1) * half], bottom[:, i * half : (i + 1) * half]], axis=1
            )
    flat[pl.ds(PAIRS, BANDS, stride=SLOT_ROWS), :] = notes
    out[...] = flat[...].astype(BF16)
    table_copy.wait()


def synthesis_kernel(
    arrived, table, basis, grid_out, share_out,
    flat, sorted_buf, series, partial_buf, turned,
):
    flat[...] = arrived[...].astype(F32)
    notes = flat[pl.ds(PAIRS, BANDS, stride=SLOT_ROWS), :]
    keep = notes[0:1, KEEP_LANE : KEEP_LANE + 1]
    target = lax.broadcasted_iota(jnp.int32, (BANDS, LOWS), 1).astype(F32)
    sources, hits = [], []
    for p in range(0, PAIRS, 2):
        couple = [flat[pl.ds(p + i, BANDS, stride=SLOT_ROWS), :] for i in range(2)]
        sources.append(jnp.concatenate(couple, axis=0).T.astype(BF16))
    for p in range(PAIRS):
        place = DIGIT * notes[:, p : p + 1] + notes[:, PAIRS + p : PAIRS + p + 1]
        hits.append(jnp.where(target == place, 1.0, 0.0).astype(BF16))
    by_wave = jnp.dot(
        jnp.concatenate(sources, axis=1),
        jnp.concatenate(hits, axis=0),
        preferred_element_type=F32,
    )
    for a in range(LOWS // BLK):
        sorted_buf[a] = by_wave[:, a * BLK : (a + 1) * BLK]
        for h in range(2):
            for c in range(2):
                for r in range(2):
                    series[2 * h + c, a, pl.ds(r, FIELDS, stride=2), :] = sorted_buf[
                        a, pl.ds(r * 64 + h * 32 + c, FIELDS, stride=2), :
                    ]
    first = lax.broadcasted_iota(jnp.int32, (2 * FIELDS, BLK), 1) < PER_CLASS
    real, imag = [], []
    for cls in range(RADIX):
        a = cls // 2
        b = RADIX // 2 - 1 - a
        halves = []
        for c in range(2):
            low = series[c, a]
            high = series[2 + c, b]
            halves.append(jnp.where(first, low, high) if cls % 2 == 0 else jnp.where(first, high, low))
        re, im = halves
        lhs = jnp.concatenate(
            [jnp.concatenate([re, im], axis=1), jnp.concatenate([im, -re], axis=1)], axis=0
        ).astype(BF16)
        both = jnp.dot(lhs, table[cls], preferred_element_type=F32)
        real.append(both[: 2 * FIELDS])
        imag.append(both[2 * FIELDS :])
    pieces = [None] * RADIX
    for q in range(3):
        sums = []
        for part, wave in ((real, math.cos), (imag, math.sin)):
            for odd in range(2):
                total = None
                for cls in range(odd, RADIX, 2):
                    factor = wave(2.0 * math.pi * cls * q / RADIX)
                    if abs(factor) < 1e-9:
                        continue
                    term = part[cls] if factor == 1.0 else part[cls] * factor
                    total = term if total is None else total + term
                sums.append(total)
        cos_even, cos_odd, sin_even, sin_odd = sums
        if q == 0:
            pieces[0] = cos_even + cos_odd
            pieces[5] = cos_even - cos_odd
        else:
            pieces[q] = (cos_even + cos_odd) - (sin_even + sin_odd)
            pieces[10 - q] = (cos_even + cos_odd) + (sin_even + sin_odd)
            pieces[5 - q] = (cos_even - cos_odd) + (sin_even - sin_odd)
            pieces[5 + q] = (cos_even - cos_odd) - (sin_even - sin_odd)
    second = lax.broadcasted_iota(jnp.int32, (2 * FIELDS, STEP), 0) % 2
    kept = keep > 0.5
    uppers, lowers = [], []
    for q in range(RADIX):
        upper_row = jnp.where(second == 0, pieces[q], 0.0)
        lower_row = jnp.where((second == 1) & kept, pieces[q], 0.0)
        grid_out[:, :, q * STEP : (q + 1) * STEP] = (
            (upper_row + lower_row).astype(BF16).reshape(FIELDS, 2, STEP)
        )
        uppers.append(upper_row.astype(BF16))
        lowers.append(lower_row.astype(BF16))
    lhs = jnp.concatenate(uppers + lowers, axis=1)
    rhs = basis[...].reshape(2 * LON, MODES)
    total = jnp.concatenate([jnp.dot(lhs, rhs[:, i*128:(i+1)*128], preferred_element_type=F32) for i in range(2)], axis=1)
    for i in range(MODES // BLK):
        partial_buf[i] = total[:, i * BLK : (i + 1) * BLK]
        turned[i * BLK : (i + 1) * BLK, :FIELDS] = (
            partial_buf[i, pl.ds(0, FIELDS, stride=2), :]
            + partial_buf[i, pl.ds(1, FIELDS, stride=2), :]
        ).T
    share_out[...] = jnp.concatenate(
        [turned[pl.ds(o, BANDS, stride=SHARE), :][:, :FIELDS] for o in range(SHARE)], axis=1
    )


VMEM = pl.BlockSpec(memory_space=pltpu.VMEM)
HBM = pl.BlockSpec(memory_space=pltpu.HBM)
PARAMS = pltpu.CompilerParams(vmem_limit_bytes=48 * 1024 * 1024)


def to_messages(waves, lengths, spectra, legendre, table):
    return pl.pallas_call(
        legendre_kernel,
        out_shape=(
            jax.ShapeDtypeStruct((BANDS * SLOT_ROWS, BLK), BF16),
            jax.ShapeDtypeStruct((RADIX, STEP, STEP), BF16),
        ),
        in_specs=[HBM, HBM, HBM, HBM, HBM],
        out_specs=(VMEM, VMEM),
        scratch_shapes=[
            pltpu.SMEM((PAIRS,), jnp.int32),
            pltpu.VMEM((1, BANDS), jnp.int32),
            pltpu.VMEM((FIELDS, 2, PAIRS * PAIR_LEN), BF16),
            pltpu.VMEM((HALF, PAIRS * PAIR_LEN), BF16),
            pltpu.VMEM((BANDS * SLOT_ROWS, BLK), F32),
            pltpu.SemaphoreType.DMA((2, LOADS)),
            pltpu.SemaphoreType.DMA((3,)),
        ],
        compiler_params=PARAMS,
    )(*[pltpu.with_memory_space_constraint(x, pltpu.HBM) for x in (waves, lengths, spectra, legendre, table)])


def to_grid(arrived, table, basis):
    return pl.pallas_call(
        synthesis_kernel,
        out_shape=(
            jax.ShapeDtypeStruct((FIELDS, 2, LON), BF16),
            jax.ShapeDtypeStruct((BANDS, SHARE * FIELDS), F32),
        ),
        in_specs=[VMEM, VMEM, VMEM],
        out_specs=(VMEM, VMEM),
        scratch_shapes=[
            pltpu.VMEM((BANDS * SLOT_ROWS, BLK), F32),
            pltpu.VMEM((LOWS // BLK, BLK, BLK), F32),
            pltpu.VMEM((4, LOWS // BLK, 2 * FIELDS, BLK), F32),
            pltpu.VMEM((MODES // BLK, 2 * FIELDS, BLK), F32),
            pltpu.VMEM((MODES, BLK), F32),
        ],
        compiler_params=PARAMS,
    )(arrived, table, basis)


def shards(spectra, legendre, pair_waves, band_lengths, eof_basis):
    ens, fields, levels, parts, slots = spectra.shape
    messages, table = to_messages(
        pair_waves,
        band_lengths.reshape(1, BANDS),
        spectra.reshape(FIELDS, parts, slots),
        legendre,
        jnp.asarray(wave_table()),
    )
    messages = messages.reshape(BANDS, SLOT_ROWS // 2, 2, BLK)
    arrived = lax.all_to_all(messages, ("plane", "ring"), 0, 0, tiled=True)
    arrived = arrived.reshape(BANDS * SLOT_ROWS, BLK)
    grid, shares = to_grid(arrived, table, eof_basis)
    shares = lax.all_to_all(shares, ("ring", "plane"), 0, 0, tiled=True)
    groups = lax.axis_size("mem")
    sums = jnp.broadcast_to(jnp.sum(shares, axis=0)[None], (groups, SHARE * FIELDS))
    everyone = lax.all_to_all(sums, "mem", 0, 0, tiled=True)
    everyone, sums = lax.optimization_barrier((everyone, sums))
    own = sums[0].reshape(SHARE, ens, fields * levels)
    total = jnp.sum(everyone, axis=0).reshape(SHARE, ens, fields * levels)
    mean = jnp.sum(total, axis=1, keepdims=True) / (ens * groups)
    anomaly = (own - mean).transpose(1, 2, 0).reshape(ens, fields, levels, SHARE)
    return grid.reshape(ens, fields, levels, 2, LON), anomaly


def solution(mesh):
    devices = mesh.devices.reshape(RING, BANDS // RING, -1)
    band = ("ring", "plane")
    return jax.shard_map(
        shards,
        mesh=Mesh(devices, (*band, "mem")),
        in_specs=(
            P("mem", None, None, None, band),
            P(None, band),
            P(band),
            P(),
            P(band, None, None),
        ),
        out_specs=(P("mem", None, None, band, None), P("mem", None, None, band)),
        check_vma=False,
    )
```

```python
import math

import jax
import jax.numpy as jnp
import numpy as np
from jax import lax
from jax.experimental import pallas as pl
from jax.experimental.pallas import tpu as pltpu
from jax.sharding import PartitionSpec as P

WAVE_COUNT = 1280
LON = 2560
BLK = 128
HALF = 40
BANDS = 64
PAIRS = 10
PAIR_LEN = 1408
FIELDS = 16
RADIX = 10
STEP = LON // RADIX
MODES = 256
SHARE = MODES // BANDS
SLOT_ROWS = 12
LOADS = 2
LOWS = WAVE_COUNT // 2
PER_CLASS = LOWS // RADIX
DIGIT = 128
KEEP_LANE = 2 * PAIRS
F32 = jnp.float32
BF16 = jnp.bfloat16


def wave_table():
    ladder = RADIX * np.arange(PER_CLASS)
    parts = []
    for c in range(RADIX):
        low = ladder + c
        high = WAVE_COUNT - RADIX - ladder + c
        orders = np.concatenate([low, high] if c % 2 == 0 else [high, low])
        phase = orders[:, None] * np.arange(STEP)[None, :] % LON
        angle = phase.astype(np.float32) * np.float32(2.0 * math.pi / LON)
        weight = np.where(orders == 0, 1.0, 2.0).astype(np.float32)[:, None]
        parts.append(np.concatenate([weight * np.cos(angle), -weight * np.sin(angle)]))
    return np.stack(parts).astype(jnp.bfloat16)


def legendre_kernel(
    waves_hbm, lengths_hbm, spectra_hbm, legendre_hbm, table_hbm, out, table,
    waves, lengths, spectra_buf, legendre_buf, flat, sems, small_sems,
):
    waves_copy = pltpu.make_async_copy(waves_hbm, waves, small_sems.at[0])
    lengths_copy = pltpu.make_async_copy(lengths_hbm, lengths, small_sems.at[1])
    waves_copy.start()
    lengths_copy.start()

    loads = []
    for i in range(LOADS):
        window = pl.ds(i * (PAIRS // LOADS) * PAIR_LEN, (PAIRS // LOADS) * PAIR_LEN)
        loads += [
            pltpu.make_async_copy(
                spectra_hbm.at[:, :, window], spectra_buf.at[:, :, window], sems.at[0, i]
            ),
            pltpu.make_async_copy(
                legendre_hbm.at[:, window], legendre_buf.at[:, window], sems.at[1, i]
            ),
        ]
    for load in loads:
        load.start()
    table_copy = pltpu.make_async_copy(table_hbm, table, small_sems.at[2])
    table_copy.start()
    waves_copy.wait()
    lengths_copy.wait()
    counts = lengths[...].astype(F32)
    dest = lax.broadcasted_iota(jnp.int32, (BANDS, BANDS), 0)
    other = lax.broadcasted_iota(jnp.int32, (BANDS, BANDS), 1)
    starts = jnp.sum(jnp.where(other < dest, counts, 0.0), axis=1, keepdims=True)
    own = jnp.sum(jnp.where(other == dest, counts, 0.0), axis=1, keepdims=True)
    column = lax.broadcasted_iota(jnp.int32, (BANDS, 2 * HALF), 1).astype(F32)
    picks = []
    for r in range(2):
        row = jnp.minimum(starts + r, 2 * HALF - 1.0)
        source = jnp.where(row < HALF, row, 3 * HALF - 1.0 - row)
        picks.append((column == source).astype(BF16))
    pick = jnp.concatenate(picks, axis=0)
    lane = lax.broadcasted_iota(jnp.int32, (BANDS, BLK), 1)
    notes = jnp.where(lane == KEEP_LANE, jnp.where(own > 1.0, 1.0, 0.0), 0.0)
    position = lax.broadcasted_iota(jnp.int32, (FIELDS, PAIR_LEN), 1)
    parity = lax.broadcasted_iota(jnp.int32, (HALF, PAIR_LEN), 1) % 2
    alternate = jnp.where(parity == 0, 1.0, -1.0).astype(BF16)
    flat[...] = jnp.zeros(flat.shape, F32)
    half = BLK // 2
    for p in range(PAIRS):
        if p % (PAIRS // LOADS) == 0:
            for load in loads[2 * p * LOADS // PAIRS :][:2]:
                load.wait()
        wave = waves[p]
        place = (wave % RADIX) * PER_CLASS + wave // RADIX
        notes = jnp.where(lane == p, (place // DIGIT).astype(F32), notes)
        notes = jnp.where(lane == PAIRS + p, (place % DIGIT).astype(F32), notes)
        upper = position - (WAVE_COUNT // BLK - wave // BLK) * BLK
        low = (position < WAVE_COUNT - wave).astype(F32).astype(BF16)
        high = ((upper >= 0) & (upper < wave + 1)).astype(F32).astype(BF16)
        window = slice(p * PAIR_LEN, (p + 1) * PAIR_LEN)
        coeffs = spectra_buf[:, :, window].reshape(2 * FIELDS, PAIR_LEN)
        halves = [jnp.concatenate([mask, mask], axis=0) * coeffs for mask in (low, high)]
        masked = jnp.concatenate(halves, axis=0)
        north = legendre_buf[:, window]
        rows = jnp.concatenate([north, north * alternate], axis=0)
        fourier = lax.dot_general(
            masked, rows, (((1,), (1,)), ((), ())), preferred_element_type=F32
        )
        every = ([] if p == 0 else every) + [fourier]
        if p < PAIRS - 1:
            continue
        couple = jnp.concatenate(every, axis=0).astype(BF16)
        picked = lax.dot_general(
            pick, couple, (((1,), (1,)), ((), ())), preferred_element_type=F32
        )
        top, bottom = picked[:BANDS], picked[BANDS:]
        for i in range(PAIRS):
            flat[pl.ds(i, BANDS, stride=SLOT_ROWS), :] = jnp.concatenate(
                [top[:, i * half : (i + 1) * half], bottom[:, i * half : (i + 1) * half]], axis=1
            )
    flat[pl.ds(PAIRS, BANDS, stride=SLOT_ROWS), :] = notes
    out[...] = flat[...].astype(BF16)
    table_copy.wait()


def synthesis_kernel(
    arrived, table, basis, grid_out, share_out,
    flat, sorted_buf, series, partial_buf, turned,
):
    flat[...] = arrived[...].astype(F32)
    notes = flat[pl.ds(PAIRS, BANDS, stride=SLOT_ROWS), :]
    keep = notes[0:1, KEEP_LANE : KEEP_LANE + 1]
    target = lax.broadcasted_iota(jnp.int32, (BANDS, BLK), 1).astype(F32)
    blocks = notes.T
    sources, hits = [], []
    for p in range(0, PAIRS, 2):
        couple = [flat[pl.ds(p + i, BANDS, stride=SLOT_ROWS), :] for i in range(2)]
        sources.append(jnp.concatenate(couple, axis=0).T.astype(BF16))
    for p in range(PAIRS):
        hits.append(
            jnp.where(target == notes[:, PAIRS + p : PAIRS + p + 1], 1.0, 0.0).astype(BF16)
        )
    source = jnp.concatenate(sources, axis=1)
    block = jnp.concatenate([blocks[p : p + 1, :BANDS] for p in range(PAIRS)], axis=1)
    block = jnp.broadcast_to(block, (FIELDS, LOWS))
    stacked = []
    for a in range(LOWS // BLK):
        mine = jnp.where(block == a, 1.0, 0.0).astype(BF16)
        stacked.append(source * jnp.concatenate([mine] * (BLK // FIELDS), axis=0))
    hit = jnp.concatenate(hits, axis=0)
    for a in range(LOWS // BLK):
        sorted_buf[a] = jnp.dot(stacked[a], hit, preferred_element_type=F32)
        for h in range(2):
            for c in range(2):
                for r in range(2):
                    series[2 * h + c, a, pl.ds(r, FIELDS, stride=2), :] = sorted_buf[
                        a, pl.ds(r * 64 + h * 32 + c, FIELDS, stride=2), :
                    ]
    first = lax.broadcasted_iota(jnp.int32, (2 * FIELDS, BLK), 1) < PER_CLASS
    real, imag = [], []
    for cls in range(RADIX):
        a = cls // 2
        b = RADIX // 2 - 1 - a
        halves = []
        for c in range(2):
            low = series[c, a]
            high = series[2 + c, b]
            halves.append(jnp.where(first, low, high) if cls % 2 == 0 else jnp.where(first, high, low))
        re, im = halves
        lhs = jnp.concatenate(
            [jnp.concatenate([re, im], axis=1), jnp.concatenate([im, -re], axis=1)], axis=0
        ).astype(BF16)
        both = jnp.dot(lhs, table[cls], preferred_element_type=F32)
        real.append(both[: 2 * FIELDS])
        imag.append(both[2 * FIELDS :])
    pieces = [None] * RADIX
    for q in range(3):
        sums = []
        for part, wave in ((real, math.cos), (imag, math.sin)):
            for odd in range(2):
                total = None
                for cls in range(odd, RADIX, 2):
                    factor = wave(2.0 * math.pi * cls * q / RADIX)
                    if abs(factor) < 1e-9:
                        continue
                    term = part[cls] if factor == 1.0 else part[cls] * factor
                    total = term if total is None else total + term
                sums.append(total)
        cos_even, cos_odd, sin_even, sin_odd = sums
        if q == 0:
            pieces[0] = cos_even + cos_odd
            pieces[5] = cos_even - cos_odd
        else:
            pieces[q] = (cos_even + cos_odd) - (sin_even + sin_odd)
            pieces[10 - q] = (cos_even + cos_odd) + (sin_even + sin_odd)
            pieces[5 - q] = (cos_even - cos_odd) + (sin_even - sin_odd)
            pieces[5 + q] = (cos_even - cos_odd) - (sin_even - sin_odd)
    second = lax.broadcasted_iota(jnp.int32, (2 * FIELDS, STEP), 0) % 2
    kept = keep > 0.5
    uppers, lowers = [], []
    for q in range(RADIX):
        upper_row = jnp.where(second == 0, pieces[q], 0.0)
        lower_row = jnp.where((second == 1) & kept, pieces[q], 0.0)
        grid_out[:, :, q * STEP : (q + 1) * STEP] = (
            (upper_row + lower_row).astype(BF16).reshape(FIELDS, 2, STEP)
        )
        uppers.append(upper_row.astype(BF16))
        lowers.append(lower_row.astype(BF16))
    lhs = jnp.concatenate(uppers + lowers, axis=1)
    rhs = basis[...].reshape(2 * LON, MODES)
    total = jnp.concatenate([sum(jnp.dot(lhs[:, k*1280:(k+1)*1280], rhs[k*1280:(k+1)*1280, i*128:(i+1)*128], preferred_element_type=F32) for k in range(4)) for i in range(2)], axis=1)
    for i in range(MODES // BLK):
        partial_buf[i] = total[:, i * BLK : (i + 1) * BLK]
        turned[i * BLK : (i + 1) * BLK, :FIELDS] = (
            partial_buf[i, pl.ds(0, FIELDS, stride=2), :]
            + partial_buf[i, pl.ds(1, FIELDS, stride=2), :]
        ).T
    share_out[...] = jnp.concatenate(
        [turned[pl.ds(o, BANDS, stride=SHARE), :][:, :FIELDS] for o in range(SHARE)], axis=1
    )


VMEM = pl.BlockSpec(memory_space=pltpu.VMEM)
HBM = pl.BlockSpec(memory_space=pltpu.HBM)
PARAMS = pltpu.CompilerParams(vmem_limit_bytes=48 * 1024 * 1024)


def to_messages(waves, lengths, spectra, legendre, table):
    return pl.pallas_call(
        legendre_kernel,
        out_shape=(
            jax.ShapeDtypeStruct((BANDS * SLOT_ROWS, BLK), BF16),
            jax.ShapeDtypeStruct((RADIX, STEP, STEP), BF16),
        ),
        in_specs=[HBM, HBM, HBM, HBM, HBM],
        out_specs=(VMEM, VMEM),
        scratch_shapes=[
            pltpu.SMEM((PAIRS,), jnp.int32),
            pltpu.VMEM((1, BANDS), jnp.int32),
            pltpu.VMEM((FIELDS, 2, PAIRS * PAIR_LEN), BF16),
            pltpu.VMEM((HALF, PAIRS * PAIR_LEN), BF16),
            pltpu.VMEM((BANDS * SLOT_ROWS, BLK), F32),
            pltpu.SemaphoreType.DMA((2, LOADS)),
            pltpu.SemaphoreType.DMA((3,)),
        ],
        compiler_params=PARAMS,
    )(*[pltpu.with_memory_space_constraint(x, pltpu.HBM) for x in (waves, lengths, spectra, legendre, table)])


def to_grid(arrived, table, basis):
    return pl.pallas_call(
        synthesis_kernel,
        out_shape=(
            jax.ShapeDtypeStruct((FIELDS, 2, LON), BF16),
            jax.ShapeDtypeStruct((BANDS, SHARE * FIELDS), F32),
        ),
        in_specs=[VMEM, VMEM, VMEM],
        out_specs=(VMEM, VMEM),
        scratch_shapes=[
            pltpu.VMEM((BANDS * SLOT_ROWS, BLK), F32),
            pltpu.VMEM((LOWS // BLK, BLK, BLK), F32),
            pltpu.VMEM((4, LOWS // BLK, 2 * FIELDS, BLK), F32),
            pltpu.VMEM((MODES // BLK, 2 * FIELDS, BLK), F32),
            pltpu.VMEM((MODES, BLK), F32),
        ],
        compiler_params=PARAMS,
    )(arrived, table, basis)


def shards(spectra, legendre, pair_waves, band_lengths, eof_basis):
    ens, fields, levels, parts, slots = spectra.shape
    messages, table = to_messages(
        pair_waves,
        band_lengths.reshape(1, BANDS),
        spectra.reshape(FIELDS, parts, slots),
        legendre,
        jnp.asarray(wave_table()),
    )
    messages = messages.reshape(BANDS, SLOT_ROWS // 2, 2, BLK)
    arrived = lax.all_to_all(messages, "band", 0, 0, tiled=True)
    arrived = arrived.reshape(BANDS * SLOT_ROWS, BLK)
    grid, shares = to_grid(arrived, table, eof_basis)
    shares = lax.all_to_all(shares, "band", 0, 0, tiled=True)
    groups = lax.axis_size("mem")
    sums = jnp.broadcast_to(jnp.sum(shares, axis=0)[None], (groups, SHARE * FIELDS))
    everyone = lax.all_to_all(sums, "mem", 0, 0, tiled=True)
    everyone, sums = lax.optimization_barrier((everyone, sums))
    own = sums[0].reshape(SHARE, ens, fields * levels)
    total = jnp.sum(everyone, axis=0).reshape(SHARE, ens, fields * levels)
    mean = jnp.sum(total, axis=1, keepdims=True) / (ens * groups)
    anomaly = (own - mean).transpose(1, 2, 0).reshape(ens, fields, levels, SHARE)
    return grid.reshape(ens, fields, levels, 2, LON), anomaly


def solution(mesh):
    return jax.shard_map(
        shards,
        mesh=mesh,
        in_specs=(
            P("mem", None, None, None, "band"),
            P(None, "band"),
            P("band"),
            P(),
            P("band", None, None),
        ),
        out_specs=(P("mem", None, None, "band", None), P("mem", None, None, "band")),
        check_vma=False,
    )
```

```python
import math

import jax
import jax.numpy as jnp
import numpy as np
from jax import lax
from jax.experimental import pallas as pl
from jax.experimental.pallas import tpu as pltpu
from jax.sharding import Mesh
from jax.sharding import PartitionSpec as P

WAVE_COUNT = 1280
LON = 2560
BLK = 128
HALF = 40
BANDS = 64
PAIRS = 10
PAIR_LEN = 1408
FIELDS = 16
RADIX = 10
STEP = LON // RADIX
MODES = 256
SHARE = MODES // BANDS
SLOT_ROWS = 12
LOADS = 2
LOWS = WAVE_COUNT // 2
PER_CLASS = LOWS // RADIX
DIGIT = 128
KEEP_LANE = 2 * PAIRS
F32 = jnp.float32
BF16 = jnp.bfloat16


def wave_table():
    ladder = RADIX * np.arange(PER_CLASS)
    parts = []
    for c in range(RADIX):
        low = ladder + c
        high = WAVE_COUNT - RADIX - ladder + c
        orders = np.concatenate([low, high] if c % 2 == 0 else [high, low])
        phase = orders[:, None] * np.arange(STEP)[None, :] % LON
        angle = phase.astype(np.float32) * np.float32(2.0 * math.pi / LON)
        weight = np.where(orders == 0, 1.0, 2.0).astype(np.float32)[:, None]
        parts.append(np.concatenate([weight * np.cos(angle), -weight * np.sin(angle)]))
    return np.stack(parts).astype(jnp.bfloat16)


def legendre_kernel(
    waves_hbm, lengths_hbm, spectra_hbm, legendre_hbm, table_hbm, out, table,
    waves, lengths, spectra_buf, legendre_buf, flat, sems, small_sems,
):
    waves_copy = pltpu.make_async_copy(waves_hbm, waves, small_sems.at[0])
    lengths_copy = pltpu.make_async_copy(lengths_hbm, lengths, small_sems.at[1])
    waves_copy.start()
    lengths_copy.start()

    loads = []
    for i in range(LOADS):
        window = pl.ds(i * (PAIRS // LOADS) * PAIR_LEN, (PAIRS // LOADS) * PAIR_LEN)
        loads += [
            pltpu.make_async_copy(
                spectra_hbm.at[:, :, window], spectra_buf.at[:, :, window], sems.at[0, i]
            ),
            pltpu.make_async_copy(
                legendre_hbm.at[:, window], legendre_buf.at[:, window], sems.at[1, i]
            ),
        ]
    for load in loads:
        load.start()
    table_copy = pltpu.make_async_copy(table_hbm, table, small_sems.at[2])
    table_copy.start()
    waves_copy.wait()
    lengths_copy.wait()
    counts = lengths[...].astype(F32)
    order = lax.broadcasted_iota(jnp.int32, (BANDS, BANDS), 0)
    dest = order // 8 * 8 + order % 4 * 2 + order // 4 % 2
    other = lax.broadcasted_iota(jnp.int32, (BANDS, BANDS), 1)
    starts = jnp.sum(jnp.where(other < dest, counts, 0.0), axis=1, keepdims=True)
    own = jnp.sum(jnp.where(other == dest, counts, 0.0), axis=1, keepdims=True)
    column = lax.broadcasted_iota(jnp.int32, (BANDS, 2 * HALF), 1).astype(F32)
    picks = []
    for r in range(2):
        row = jnp.minimum(starts + r, 2 * HALF - 1.0)
        source = jnp.where(row < HALF, row, 3 * HALF - 1.0 - row)
        picks.append((column == source).astype(BF16))
    pick = jnp.concatenate(picks, axis=0)
    lane = lax.broadcasted_iota(jnp.int32, (BANDS, BLK), 1)
    notes = jnp.where(lane == KEEP_LANE, jnp.where(own > 1.0, 1.0, 0.0), 0.0)
    position = lax.broadcasted_iota(jnp.int32, (FIELDS, PAIR_LEN), 1)
    parity = lax.broadcasted_iota(jnp.int32, (HALF, PAIR_LEN), 1) % 2
    alternate = jnp.where(parity == 0, 1.0, -1.0).astype(BF16)
    flat[...] = jnp.zeros(flat.shape, F32)
    half = BLK // 2
    for p in range(PAIRS):
        if p % (PAIRS // LOADS) == 0:
            for load in loads[2 * p * LOADS // PAIRS :][:2]:
                load.wait()
        wave = waves[p]
        place = (wave % RADIX) * PER_CLASS + wave // RADIX
        notes = jnp.where(lane == p, (place // DIGIT).astype(F32), notes)
        notes = jnp.where(lane == PAIRS + p, (place % DIGIT).astype(F32), notes)
        upper = position - (WAVE_COUNT // BLK - wave // BLK) * BLK
        low = (position < WAVE_COUNT - wave).astype(F32).astype(BF16)
        high = ((upper >= 0) & (upper < wave + 1)).astype(F32).astype(BF16)
        window = slice(p * PAIR_LEN, (p + 1) * PAIR_LEN)
        coeffs = spectra_buf[:, :, window].reshape(2 * FIELDS, PAIR_LEN)
        halves = [jnp.concatenate([mask, mask], axis=0) * coeffs for mask in (low, high)]
        masked = jnp.concatenate(halves, axis=0)
        north = legendre_buf[:, window]
        rows = jnp.concatenate([north, north * alternate], axis=0)
        fourier = lax.dot_general(
            masked, rows, (((1,), (1,)), ((), ())), preferred_element_type=F32
        )
        every = ([] if p == 0 else every) + [fourier]
        if p < PAIRS - 1:
            continue
        couple = jnp.concatenate(every, axis=0).astype(BF16)
        picked = lax.dot_general(
            pick, couple, (((1,), (1,)), ((), ())), preferred_element_type=F32
        )
        top, bottom = picked[:BANDS], picked[BANDS:]
        for i in range(PAIRS):
            flat[pl.ds(i, BANDS, stride=SLOT_ROWS), :] = jnp.concatenate(
                [top[:, i * half : (i + 1) * half], bottom[:, i * half : (i + 1) * half]], axis=1
            )
    flat[pl.ds(PAIRS, BANDS, stride=SLOT_ROWS), :] = notes
    out[...] = flat[...].astype(BF16)
    table_copy.wait()


def synthesis_kernel(
    arrived, table, basis, grid_out, share_out,
    flat, sorted_buf, series, partial_buf, turned,
):
    flat[...] = arrived[...].astype(F32)
    notes = flat[pl.ds(PAIRS, BANDS, stride=SLOT_ROWS), :]
    keep = notes[0:1, KEEP_LANE : KEEP_LANE + 1]
    target = lax.broadcasted_iota(jnp.int32, (BANDS, BLK), 1).astype(F32)
    blocks = notes.T
    sources, hits = [], []
    for p in range(0, PAIRS, 2):
        couple = [flat[pl.ds(p + i, BANDS, stride=SLOT_ROWS), :] for i in range(2)]
        sources.append(jnp.concatenate(couple, axis=0).T.astype(BF16))
    for p in range(PAIRS):
        hits.append(
            jnp.where(target == notes[:, PAIRS + p : PAIRS + p + 1], 1.0, 0.0).astype(BF16)
        )
    source = jnp.concatenate(sources, axis=1)
    block = jnp.concatenate([blocks[p : p + 1, :BANDS] for p in range(PAIRS)], axis=1)
    block = jnp.broadcast_to(block, (FIELDS, LOWS))
    stacked = []
    for a in range(LOWS // BLK):
        mine = jnp.where(block == a, 1.0, 0.0).astype(BF16)
        stacked.append(source * jnp.concatenate([mine] * (BLK // FIELDS), axis=0))
    hit = jnp.concatenate(hits, axis=0)
    for a in range(LOWS // BLK):
        sorted_buf[a] = jnp.dot(stacked[a], hit, preferred_element_type=F32)
        for h in range(2):
            for c in range(2):
                for r in range(2):
                    series[2 * h + c, a, pl.ds(r, FIELDS, stride=2), :] = sorted_buf[
                        a, pl.ds(r * 64 + h * 32 + c, FIELDS, stride=2), :
                    ]
    first = lax.broadcasted_iota(jnp.int32, (2 * FIELDS, BLK), 1) < PER_CLASS
    real, imag = [], []
    for cls in range(RADIX):
        a = cls // 2
        b = RADIX // 2 - 1 - a
        halves = []
        for c in range(2):
            low = series[c, a]
            high = series[2 + c, b]
            halves.append(jnp.where(first, low, high) if cls % 2 == 0 else jnp.where(first, high, low))
        re, im = halves
        lhs = jnp.concatenate(
            [jnp.concatenate([re, im], axis=1), jnp.concatenate([im, -re], axis=1)], axis=0
        ).astype(BF16)
        both = jnp.dot(lhs, table[cls], preferred_element_type=F32)
        real.append(both[: 2 * FIELDS])
        imag.append(both[2 * FIELDS :])
    pieces = [None] * RADIX
    for q in range(3):
        sums = []
        for part, wave in ((real, math.cos), (imag, math.sin)):
            for odd in range(2):
                total = None
                for cls in range(odd, RADIX, 2):
                    factor = wave(2.0 * math.pi * cls * q / RADIX)
                    if abs(factor) < 1e-9:
                        continue
                    term = part[cls] if factor == 1.0 else part[cls] * factor
                    total = term if total is None else total + term
                sums.append(total)
        cos_even, cos_odd, sin_even, sin_odd = sums
        if q == 0:
            pieces[0] = cos_even + cos_odd
            pieces[5] = cos_even - cos_odd
        else:
            pieces[q] = (cos_even + cos_odd) - (sin_even + sin_odd)
            pieces[10 - q] = (cos_even + cos_odd) + (sin_even + sin_odd)
            pieces[5 - q] = (cos_even - cos_odd) + (sin_even - sin_odd)
            pieces[5 + q] = (cos_even - cos_odd) - (sin_even - sin_odd)
    second = lax.broadcasted_iota(jnp.int32, (2 * FIELDS, STEP), 0) % 2
    kept = keep > 0.5
    uppers, lowers = [], []
    for q in range(RADIX):
        upper_row = jnp.where(second == 0, pieces[q], 0.0)
        lower_row = jnp.where((second == 1) & kept, pieces[q], 0.0)
        grid_out[:, :, q * STEP : (q + 1) * STEP] = (
            (upper_row + lower_row).astype(BF16).reshape(FIELDS, 2, STEP)
        )
        uppers.append(upper_row.astype(BF16))
        lowers.append(lower_row.astype(BF16))
    lhs = jnp.concatenate(uppers + lowers, axis=1)
    rhs = basis[...].reshape(2 * LON, MODES)
    total = jnp.concatenate([sum(jnp.dot(lhs[:, k*1280:(k+1)*1280], rhs[k*1280:(k+1)*1280, i*128:(i+1)*128], preferred_element_type=F32) for k in range(4)) for i in range(2)], axis=1)
    for i in range(MODES // BLK):
        partial_buf[i] = total[:, i * BLK : (i + 1) * BLK]
        turned[i * BLK : (i + 1) * BLK, :FIELDS] = (
            partial_buf[i, pl.ds(0, FIELDS, stride=2), :]
            + partial_buf[i, pl.ds(1, FIELDS, stride=2), :]
        ).T
    share_out[...] = jnp.concatenate(
        [turned[pl.ds(o, BANDS, stride=SHARE), :][:, :FIELDS] for o in range(SHARE)], axis=1
    )


VMEM = pl.BlockSpec(memory_space=pltpu.VMEM)
HBM = pl.BlockSpec(memory_space=pltpu.HBM)
PARAMS = pltpu.CompilerParams(vmem_limit_bytes=48 * 1024 * 1024)


def to_messages(waves, lengths, spectra, legendre, table):
    return pl.pallas_call(
        legendre_kernel,
        out_shape=(
            jax.ShapeDtypeStruct((BANDS * SLOT_ROWS, BLK), BF16),
            jax.ShapeDtypeStruct((RADIX, STEP, STEP), BF16),
        ),
        in_specs=[HBM, HBM, HBM, HBM, HBM],
        out_specs=(VMEM, VMEM),
        scratch_shapes=[
            pltpu.SMEM((PAIRS,), jnp.int32),
            pltpu.VMEM((1, BANDS), jnp.int32),
            pltpu.VMEM((FIELDS, 2, PAIRS * PAIR_LEN), BF16),
            pltpu.VMEM((HALF, PAIRS * PAIR_LEN), BF16),
            pltpu.VMEM((BANDS * SLOT_ROWS, BLK), F32),
            pltpu.SemaphoreType.DMA((2, LOADS)),
            pltpu.SemaphoreType.DMA((3,)),
        ],
        compiler_params=PARAMS,
    )(*[pltpu.with_memory_space_constraint(x, pltpu.HBM) for x in (waves, lengths, spectra, legendre, table)])


def to_grid(arrived, table, basis):
    return pl.pallas_call(
        synthesis_kernel,
        out_shape=(
            jax.ShapeDtypeStruct((FIELDS, 2, LON), BF16),
            jax.ShapeDtypeStruct((BANDS, SHARE * FIELDS), F32),
        ),
        in_specs=[VMEM, VMEM, VMEM],
        out_specs=(VMEM, VMEM),
        scratch_shapes=[
            pltpu.VMEM((BANDS * SLOT_ROWS, BLK), F32),
            pltpu.VMEM((LOWS // BLK, BLK, BLK), F32),
            pltpu.VMEM((4, LOWS // BLK, 2 * FIELDS, BLK), F32),
            pltpu.VMEM((MODES // BLK, 2 * FIELDS, BLK), F32),
            pltpu.VMEM((MODES, BLK), F32),
        ],
        compiler_params=PARAMS,
    )(arrived, table, basis)


def shards(spectra, legendre, pair_waves, band_lengths, eof_basis):
    ens, fields, levels, parts, slots = spectra.shape
    messages, table = to_messages(
        pair_waves,
        band_lengths.reshape(1, BANDS),
        spectra.reshape(FIELDS, parts, slots),
        legendre,
        jnp.asarray(wave_table()),
    )
    messages = messages.reshape(BANDS, SLOT_ROWS // 2, 2, BLK)
    arrived = lax.all_to_all(messages, ("z", "core", "x"), 0, 0, tiled=True)
    arrived = arrived.reshape(BANDS * SLOT_ROWS, BLK)
    grid, shares = to_grid(arrived, table, eof_basis)
    shares = lax.all_to_all(shares, ("z", "x", "core"), 0, 0, tiled=True)
    groups = lax.axis_size("mem")
    sums = jnp.broadcast_to(jnp.sum(shares, axis=0)[None], (groups, SHARE * FIELDS))
    everyone = lax.all_to_all(sums, "mem", 0, 0, tiled=True)
    everyone, sums = lax.optimization_barrier((everyone, sums))
    own = sums[0].reshape(SHARE, ens, fields * levels)
    total = jnp.sum(everyone, axis=0).reshape(SHARE, ens, fields * levels)
    mean = jnp.sum(total, axis=1, keepdims=True) / (ens * groups)
    anomaly = (own - mean).transpose(1, 2, 0).reshape(ens, fields, levels, SHARE)
    return grid.reshape(ens, fields, levels, 2, LON), anomaly


def solution(mesh):
    band = ("z", "x", "core")
    return jax.shard_map(
        shards,
        mesh=Mesh(mesh.devices.reshape(8, 4, 2, -1), (*band, "mem")),
        in_specs=(
            P("mem", None, None, None, band),
            P(None, band),
            P(band),
            P(),
            P(band, None, None),
        ),
        out_specs=(P("mem", None, None, band, None), P("mem", None, None, band)),
        check_vma=False,
    )
```
